32 devices in a mesh: sector: 8 (over y, x, core), term: 4 (over z).
Axes of the slice: x: 2, y: 2, z: 4, core: 2. Of those that a mesh axis runs over, the one named last changes fastest.
Arguments:
- x_start: float32 [8, 384, 384], P('sector', 'term'), may hold values from -6 to 6
- x_prev: float32 [8, 384, 384], P('sector', 'term'), may hold values from -6 to 6
- precond: float32 [8, 384, 384], P('sector', 'term'), may hold values from 0.5 to 6
- left_env: bfloat16 [256, 384, 384], P(('sector', 'term')), may hold values from -0.20412415 to 1.2041241
- right_env: bfloat16 [256, 384, 384], P(('sector', 'term')), may hold values from -0.20412415 to 1.2041241
- triples: int32 [640, 4], P(('sector', 'term')), may hold values from 0 to 63, as said below
- trip_count: int32 [8, 4], P('sector', 'term'), may hold values from 5 to 20, as said below
- term_coef: float32 [64], replicated, may hold values from 0.25 to 1
- lanczos_beta: float32 [3], replicated, may hold values from 0.3 to 1.2
- block_owner: int32 [8], replicated, may hold values from 0 to 7, each once
Outputs:
- final_vector: float32 [8, 384, 384], P('sector', 'term')
- rayleigh: float32 [3], replicated
The draws below stay inside these ranges and needn't reach their ends.
Inputs may be any that keep to these rules, and one draw needn't show every extreme that they name: `triples`: Columns: a left slot below 8, a wavefunction block id below 8, a right slot below 8, an operator term below 64. `trip_count`: some device has exactly 20 live triples in every draw. `block_owner`: each sector index holds exactly one block.
All inputs are finite; a program needn't handle non-finite values.
Results may differ from the reference program's by a relative error of at most 0.006.
Values may be sent and summed in bfloat16 or wider, within the bound.
No kernel may reach another device: no remote copies, remote signals or barrier semaphores. Data moves between devices by JAX's collectives and lax.ppermute only.
A program may use at most 64 MiB of HBM per device.

```python
import math
import jax
import jax.numpy as jnp
from jax import lax

B = 384
TRIP = 20
ENV_DEV = 8
TERMS = 64
APPS = 3
WBLK = 8
N_SECTOR = 8
N_TERM = 4


def draw_precond(key, part):
    base = jax.random.uniform(key, (N_SECTOR, B, B), jnp.float32)
    local = jnp.exp(jnp.log(0.5) + base * jnp.log(4.0))
    rising = 1.0 + 2.0 * jnp.arange(N_SECTOR, dtype=jnp.float32) / max(N_SECTOR - 1, 1)
    return local * rising[:, None, None]


def identity_blocks(count):
    rows = jnp.arange(B, dtype=jnp.int32)
    single = jnp.where(rows[:, None] == rows[None, :], 1.0, 0.0).astype(jnp.float32)
    return jnp.broadcast_to(single[None], (count, B, B))


def draw_left_env(key, part):
    count = N_SECTOR * N_TERM * ENV_DEV
    spread = 1.0 / math.sqrt(B)
    inner = jax.random.fold_in(key, 31)
    noise = jnp.clip(jax.random.normal(inner, (count, B, B), jnp.float32), -3.0, 3.0) * spread
    return (identity_blocks(count) + noise).astype(jnp.bfloat16)


def draw_right_env(key, part):
    count = N_SECTOR * N_TERM * ENV_DEV
    spread = 1.0 / math.sqrt(B)
    inner = jax.random.fold_in(key, 32)
    noise = jnp.clip(jax.random.normal(inner, (count, B, B), jnp.float32), -3.0, 3.0) * spread
    return (identity_blocks(count) + noise).astype(jnp.bfloat16)


def draw_triples(key, part):
    total_rows = N_SECTOR * N_TERM * TRIP
    left_slot = jax.random.randint(jax.random.fold_in(key, 11), (total_rows,), 0, ENV_DEV)
    wave_block = jax.random.randint(jax.random.fold_in(key, 12), (total_rows,), 0, N_SECTOR)
    right_slot = jax.random.randint(jax.random.fold_in(key, 13), (total_rows,), 0, ENV_DEV)
    term_index = jax.random.randint(jax.random.fold_in(key, 14), (total_rows,), 0, TERMS)
    return jnp.stack([left_slot, wave_block, right_slot, term_index], axis=1).astype(jnp.int32)


def draw_trip_count(key, part):
    lowest = max(1, TRIP // 4)
    spread = TRIP - lowest
    first = jax.random.randint(jax.random.fold_in(key, 21), (N_SECTOR, N_TERM), 0, spread + 1)
    second = jax.random.randint(jax.random.fold_in(key, 22), (N_SECTOR, N_TERM), 0, spread + 1)
    counts = lowest + first * second // max(spread, 1)
    pick_sector = jax.random.randint(jax.random.fold_in(key, 23), (), 0, N_SECTOR)
    pick_term = jax.random.randint(jax.random.fold_in(key, 24), (), 0, N_TERM)
    counts = counts.at[pick_sector, pick_term].set(TRIP)
    return counts.astype(jnp.int32)


def shard_levels(own_key, extent, shards, least, high):
    def one(dim, shards_of):
        steps = jax.random.uniform(jax.random.fold_in(jax.random.fold_in(own_key, 6), dim), (shards_of,), jnp.float32, least / len(shards), high / len(shards))
        return jnp.repeat(jnp.exp(steps), extent[dim] // shards_of).reshape((-1,) + (1,) * (len(extent) - dim - 1))

    level = one(*shards[0])
    for cut in shards[1:]:
        level = level * one(*cut)
    return level


def centred(key, shape, width, limit, shards=(), held_as=jnp.bfloat16):
    drawn = width * jax.random.normal(key, shape, jnp.float32)
    if shards:
        drawn = drawn * shard_levels(key, shape, shards, -0.22, 0.18)
    return jnp.clip(drawn, -limit, limit).astype(held_as)


def setup_inputs(seed: int = 0) -> dict:
    seeds = jax.random.split(jax.random.key(seed), 11)
    x_start = centred(seeds[0], (WBLK, B, B), 1.0, 6.0, ((0, 8), (1, 4)), jnp.float32)
    x_prev = centred(seeds[1], (WBLK, B, B), 1.0, 6.0, ((0, 8), (1, 4)), jnp.float32)
    precond = draw_precond(jax.random.fold_in(seeds[10], 71), 0)
    left_env = draw_left_env(jax.random.fold_in(seeds[10], 71), 0)
    right_env = draw_right_env(jax.random.fold_in(seeds[10], 71), 0)
    triples = draw_triples(jax.random.fold_in(seeds[10], 71), 0)
    trip_count = draw_trip_count(jax.random.fold_in(seeds[10], 71), 0)
    term_coef = jnp.clip(jax.random.uniform(seeds[7], (TERMS,), jnp.float32, 0.25, 1.0), 0.25, 1.0)
    lanczos_beta = jnp.clip(jax.random.uniform(seeds[8], (APPS,), jnp.float32, 0.3, 1.2), 0.3, 1.2)
    block_owner = jax.random.permutation(seeds[9], WBLK).astype(jnp.int32)
    return dict(x_start=x_start, x_prev=x_prev, precond=precond, left_env=left_env, right_env=right_env, triples=triples, trip_count=trip_count, term_coef=term_coef, lanczos_beta=lanczos_beta, block_owner=block_owner)


EPSILON = 1e-06

def reference(x_start, x_prev, precond, left_env, right_env, triples, trip_count, term_coef, lanczos_beta, block_owner):
    normaliser = 1.0 / math.sqrt(N_TERM * TRIP)
    per_sector = N_TERM * TRIP
    left_sector = left_env.reshape(N_SECTOR, N_TERM * ENV_DEV, B, B)
    right_sector = right_env.reshape(N_SECTOR, N_TERM * ENV_DEV, B, B)
    triple_rows = triples.reshape(N_SECTOR, per_sector, 4)
    slot_index = jnp.arange(per_sector, dtype=jnp.int32)
    slot_term = slot_index // TRIP
    is_live = (slot_index % TRIP)[None, :] < jnp.repeat(trip_count, TRIP, axis=1)
    weights_live = jnp.where(is_live, term_coef[triple_rows[:, :, 3]], jnp.zeros((), term_coef.dtype))

    def apply_hamiltonian(wave):

        def sector_image(operands):
            left_blocks, right_blocks, rows_here, coef_here = operands
            left_index = (slot_term * ENV_DEV + rows_here[:, 0]).astype(jnp.int32)
            right_index = (slot_term * ENV_DEV + rows_here[:, 2]).astype(jnp.int32)
            left_taken = left_blocks[left_index].astype(jnp.float32)
            wave_taken = wave[block_owner[rows_here[:, 1]]].astype(jnp.float32)
            middle = jnp.einsum('kij,kjl->kil', left_taken, wave_taken, precision=lax.Precision.HIGHEST)
            middle = lax.optimization_barrier(middle.astype(jnp.bfloat16)).astype(jnp.float32)
            right_taken = right_blocks[right_index].astype(jnp.float32)
            return jnp.einsum('kil,klm->im', middle * coef_here[:, None, None], right_taken, precision=lax.Precision.HIGHEST)
        return lax.map(sector_image, (left_sector, right_sector, triple_rows, weights_live)) * normaliser
    current, previous = (x_start, x_prev)
    quotients = []
    for position in range(APPS):
        applied = apply_hamiltonian(current.astype(jnp.bfloat16))
        quotient = jnp.sum(current * applied) / jnp.sum(current * current)
        residual = applied - quotient * current - lanczos_beta[position] * previous
        scaled = precond * residual
        following = scaled / jnp.sqrt(jnp.mean(scaled * scaled) + EPSILON)
        previous, current = (current, following)
        quotients.append(quotient)
    return (current, jnp.stack(quotients))
```

```python
import functools
import math

import jax
import jax.numpy as jnp
from jax import lax
from jax.experimental import pallas as pl
from jax.experimental.pallas import tpu as pltpu
from jax.sharding import PartitionSpec as P

APPS = 3
EPSILON = 1e-06

F32 = jnp.float32
BF16 = jnp.bfloat16
SUBLANES = 8
LANES = 128

SCALARS = pl.BlockSpec(memory_space=pltpu.SMEM)
NEAR = pl.BlockSpec(memory_space=pltpu.VMEM)
ANYWHERE = pl.BlockSpec(memory_space=pl.ANY)


def exchange(array, axis, flip):
    count = lax.axis_size(axis)
    return lax.ppermute(array, axis, [(i, i ^ flip) for i in range(count)])


def tree(parts):
    while len(parts) > 1:
        parts = [parts[i] + parts[i + 1] for i in range(0, len(parts), 2)]
    return parts[0]


def sum_everywhere(values, sectors, term_count):
    values = values + exchange(values, "sector", 1)
    values = tree([values] + [exchange(values, "sector", f) for f in range(2, sectors, 2)])
    return tree([values] + [exchange(values, "term", f) for f in range(1, term_count)])


def gather_term(rows, term_count):
    parts = [rows] + [exchange(rows, "term", flip) for flip in range(1, term_count)]
    me = lax.axis_index("term")
    ordered = []
    for index in range(term_count):
        chosen = parts[0]
        for flip in range(1, term_count):
            chosen = jnp.where((me ^ flip) == index, parts[flip], chosen)
        ordered.append(chosen)
    return jnp.concatenate(ordered, axis=0)


def gather_sector(block, sectors):
    own_core = [block] + [exchange(block, "sector", flip) for flip in range(2, sectors, 2)]
    blocks = []
    for held in own_core:
        blocks += [held, exchange(held, "sector", 1)]
    return blocks


def fold(values):
    rows, columns = values.shape
    down = jnp.sum(values.reshape(rows // SUBLANES, SUBLANES, columns), axis=0)
    return tree_any([down[:, i : i + LANES] for i in range(0, columns, LANES)])


def tree_any(parts):
    total = parts[0]
    for part in parts[1:]:
        total = total + part
    return total


def apply_kernel(
    sectors, term_count, unroll, normaliser, triples, owner, live, coef, place, left, right, *rest
):
    waves = rest[:sectors]
    chunks = rest[sectors : sectors + term_count]
    inner, wave, total, halves, image, sems = rest[sectors + term_count :]
    slots = triples.shape[0]
    size = left.shape[1]
    envs = right.shape[0]
    share = size // term_count
    copies = [
        pltpu.make_async_copy(waves[j], wave.at[j], sems.at[j]) for j in range(sectors)
    ]
    for copy in copies:
        copy.start()
    for env in range(envs):
        total[env] = jnp.zeros((size, size), F32)
    for copy in copies:
        copy.wait()

    def one(k):
        weight = jnp.where(k < live[0, 0], coef[triples[k, 3]], 0.0) * normaliser
        source = owner[triples[k, 1]] ^ place[0]
        slot = triples[k, 2]
        total[slot] += weight * jnp.dot(
            left[triples[k, 0]], wave[source], preferred_element_type=F32
        )

    def step(i, carry):
        for u in range(unroll):
            one(i * unroll + u)
        return carry

    lax.fori_loop(0, slots // unroll, step, 0)
    for env in range(envs):
        halves[:, env * size : (env + 1) * size] = total[env].astype(BF16)
    flat = right[...].reshape(envs * size, size)
    image[...] = jnp.dot(halves[...], flat, preferred_element_type=F32)
    for flip in range(term_count):
        start = pl.multiple_of((place[1] ^ flip) * share, SUBLANES)
        chunks[flip][...] = image[pl.ds(start, share), :].astype(chunks[flip].dtype)
    inner[...] = fold(wave[0].astype(F32) * image[...])


def apply_local(triples, owner, live, coef, place, left, right, waves, term_count):
    sectors = len(waves)
    slots = triples.shape[0]
    envs, size, _ = left.shape
    share = size // term_count
    unroll = next(u for u in (4, 2, 1) if slots % u == 0)
    normaliser = 1.0 / math.sqrt(term_count * slots)
    chunk_types = [F32] + [BF16] * (term_count - 1)
    result = pl.pallas_call(
        functools.partial(apply_kernel, sectors, term_count, unroll, normaliser),
        out_shape=[jax.ShapeDtypeStruct((share, size), kind) for kind in chunk_types]
        + [jax.ShapeDtypeStruct((SUBLANES, LANES), F32)],
        in_specs=[SCALARS] * 5 + [NEAR] * 2 + [ANYWHERE] * sectors,
        out_specs=[NEAR] * (term_count + 1),
        scratch_shapes=[
            pltpu.VMEM((sectors, size, size), BF16),
            pltpu.VMEM((envs, size, size), F32),
            pltpu.VMEM((size, envs * size), BF16),
            pltpu.VMEM((size, size), F32),
            pltpu.SemaphoreType.DMA((sectors,)),
        ],
        name="apply_triples",
        cost_estimate=pl.CostEstimate(
            flops=2 * size**3 * (slots + envs),
            bytes_accessed=2 * size * size * (2 * envs + sectors + 1),
            transcendentals=0,
        ),
        compiler_params=pltpu.CompilerParams(vmem_limit_bytes=32 << 20),
    )(triples, owner, live, coef, place, left, right, *waves)
    return result[:term_count], result[term_count]


def first_kernel(rows, wave, overlap, square):
    held = rows[...]
    rounded = held.astype(BF16)
    wave[...] = rounded
    overlap[...] = fold(held * rounded.astype(F32))
    square[...] = fold(held * held)


def first(rows):
    tile = jax.ShapeDtypeStruct((SUBLANES, LANES), F32)
    return pl.pallas_call(
        first_kernel,
        out_shape=[jax.ShapeDtypeStruct(rows.shape, BF16), tile, tile],
        in_specs=[NEAR],
        out_specs=[NEAR] * 3,
        name="first_wave",
    )(rows)


def image_of(chunks):
    return tree_any([chunk[...].astype(F32) for chunk in chunks])


def advance_kernel(
    cell_count, normalised, count, beta, scale, sums, current, previous, diagonal, *rest
):
    chunks = rest[:count]
    following, wave, overlap, square, quotient, scale_out = rest[count:]
    applied = image_of(chunks)
    ratio = jnp.sum(sums[:SUBLANES], keepdims=True) / jnp.sum(
        sums[SUBLANES : 2 * SUBLANES], keepdims=True
    )
    if normalised:
        mean = jnp.sum(sums[2 * SUBLANES :], keepdims=True) / cell_count
        inverse = 1.0 / jnp.sqrt(mean + EPSILON)
    else:
        inverse = jnp.ones((1, 1), F32)
    held = current[...]
    residual = (applied - ratio * held) * inverse - (beta[0] * scale[:1, :1]) * previous[...]
    scaled = diagonal[...] * residual
    rounded = scaled.astype(BF16)
    following[...] = scaled
    wave[...] = rounded
    overlap[...] = fold(scaled * rounded.astype(F32))
    square[...] = fold(scaled * scaled)
    quotient[...] = jnp.broadcast_to(ratio, quotient.shape)
    scale_out[...] = jnp.broadcast_to(inverse, scale_out.shape)


def advance(cell_count, normalised, beta, scale, sums, current, previous, diagonal, chunks):
    tile = jax.ShapeDtypeStruct((SUBLANES, LANES), F32)
    return pl.pallas_call(
        functools.partial(advance_kernel, cell_count, normalised, len(chunks)),
        out_shape=[
            jax.ShapeDtypeStruct(current.shape, F32),
            jax.ShapeDtypeStruct(current.shape, BF16),
            tile,
            tile,
            tile,
            tile,
        ],
        in_specs=[SCALARS] + [NEAR] * (5 + len(chunks)),
        out_specs=[NEAR] * 6,
        name="advance",
    )(beta, scale, sums, current, previous, diagonal, *chunks)


PRODUCTS = 8


def closing_kernel(count, beta, scale, current, previous, diagonal, *rest):
    chunks = rest[:count]
    applied_out, products = rest[count:]
    applied = image_of(chunks)
    applied_out[...] = applied
    held = current[...]
    weight = diagonal[...]
    direct = weight * applied
    turned = weight * held
    older = weight * ((beta[0] * scale[:1, :1]) * previous[...])
    pairs = (
        (held, applied),
        (held, held),
        (direct, direct),
        (direct, turned),
        (turned, turned),
        (direct, older),
        (turned, older),
        (older, older),
    )
    for i, (a, b) in enumerate(pairs):
        products[i * SUBLANES : (i + 1) * SUBLANES, :] = fold(a * b)


def closing(beta, scale, current, previous, diagonal, chunks):
    return pl.pallas_call(
        functools.partial(closing_kernel, len(chunks)),
        out_shape=[
            jax.ShapeDtypeStruct(current.shape, F32),
            jax.ShapeDtypeStruct((PRODUCTS * SUBLANES, LANES), F32),
        ],
        in_specs=[SCALARS] + [NEAR] * (4 + len(chunks)),
        out_specs=[NEAR] * 2,
        name="closing_products",
    )(beta, scale, current, previous, diagonal, *chunks)


def final_kernel(
    cell_count, beta, scale, sums, square, applied, current, previous, diagonal, out, quotient
):
    def total(i):
        return jnp.sum(sums[i * SUBLANES : (i + 1) * SUBLANES], keepdims=True)

    ratio = total(0) / total(1)
    inverse = 1.0 / jnp.sqrt(total(1) / cell_count + EPSILON)
    quotient[...] = jnp.broadcast_to(ratio, quotient.shape)
    inner = total(2) - 2.0 * ratio * total(3) + ratio * ratio * total(4)
    mixed = total(5) - ratio * total(6)
    squares = inverse * inverse * inner - 2.0 * inverse * mixed + total(7)
    norm = 1.0 / jnp.sqrt(squares / cell_count + EPSILON)
    residual = (applied[...] - ratio * current[...]) * inverse
    residual = residual - (beta[0] * scale[:1, :1]) * previous[...]
    out[...] = diagonal[...] * residual * norm


def final(cell_count, beta, scale, sums, square, applied, current, previous, diagonal):
    return pl.pallas_call(
        functools.partial(final_kernel, cell_count),
        out_shape=[
            jax.ShapeDtypeStruct(current.shape, F32),
            jax.ShapeDtypeStruct((SUBLANES, LANES), F32),
        ],
        in_specs=[SCALARS] + [NEAR] * 7,
        out_specs=[NEAR] * 2,
        name="final_vector",
    )(beta, scale, sums, square, applied, current, previous, diagonal)


def local(
    x_start,
    x_prev,
    precond,
    left_env,
    right_env,
    triples,
    trip_count,
    term_coef,
    lanczos_beta,
    block_owner,
):
    sectors = lax.axis_size("sector")
    term_count = lax.axis_size("term")
    size = left_env.shape[1]
    cell_count = sectors * size * size
    place = jnp.stack([lax.axis_index("sector"), lax.axis_index("term")]).astype(jnp.int32)

    current, previous, diagonal = x_start[0], x_prev[0], precond[0]
    rows, overlap, square = first(current)
    scale = jnp.ones((SUBLANES, LANES), F32)
    quotients = []
    for position in range(APPS):
        beta = lanczos_beta[position : position + 1]
        waves = gather_sector(gather_term(rows, term_count), sectors)
        chunks, inner = apply_local(
            triples, block_owner, trip_count, term_coef, place, left_env, right_env, waves, term_count
        )
        arrived = [chunks[0]] + [
            exchange(chunks[flip], "term", flip) for flip in range(1, term_count)
        ]
        if position < APPS - 1:
            sums = sum_everywhere(
                jnp.concatenate([inner, overlap, square]), sectors, term_count
            )
            following, rows, overlap, square, quotient, scale_new = advance(
                cell_count, position > 0, beta, scale, sums, current, previous, diagonal, arrived
            )
            previous, current, scale = current, following, scale_new
        else:
            applied, products = closing(beta, scale, current, previous, diagonal, arrived)
            sums = sum_everywhere(products, sectors, term_count)
            current, quotient = final(
                cell_count, beta, scale, sums, square, applied, current, previous, diagonal
            )
        quotients.append(quotient[0, 0])
    return current[None], jnp.stack(quotients)


def solution(mesh):
    placed = (
        P("sector", "term", None),
        P("sector", "term", None),
        P("sector", "term", None),
        P(("sector", "term"), None, None),
        P(("sector", "term"), None, None),
        P(("sector", "term"), None),
        P("sector", "term"),
        P(),
        P(),
        P(),
    )
    return jax.shard_map(
        local,
        mesh=mesh,
        in_specs=placed,
        out_specs=(P("sector", "term", None), P()),
        check_vma=False,
    )
```

```python
import functools
import math

import jax
import jax.numpy as jnp
from jax import lax
from jax.experimental import pallas as pl
from jax.experimental.pallas import tpu as pltpu
from jax.sharding import PartitionSpec as P


APPS = 3
EPSILON = 1e-06

F32 = jnp.float32
BF16 = jnp.bfloat16
SUBLANES = 8
HEAD = 16
LANES = 128

SCALARS = pl.BlockSpec(memory_space=pltpu.SMEM)
NEAR = pl.BlockSpec(memory_space=pltpu.VMEM)
FAR = pl.BlockSpec(memory_space=pltpu.HBM)
SMALL_CALL = pltpu.CompilerParams(vmem_limit_bytes=4 << 20)


def exchange(array, axis, flip):
    count = lax.axis_size(axis)
    return lax.ppermute(array, axis, [(i, i ^ flip) for i in range(count)])


def tree(parts):
    while len(parts) > 1:
        parts = [parts[i] + parts[i + 1] for i in range(0, len(parts), 2)]
    return parts[0]


def sum_term(values, term_count):
    flip = 1
    while flip < term_count:
        values = values + exchange(values, "term", flip)
        flip *= 2
    return values


def gather_ordered(rows, term_count):
    parts = [rows]
    for flip in range(1, term_count):
        parts.append(exchange(rows, "term", flip))
    me = lax.axis_index("term")
    ordered = []
    for index in range(term_count):
        chosen = parts[0]
        for flip in range(1, term_count):
            chosen = jnp.where((me ^ flip) == index, parts[flip], chosen)
        ordered.append(chosen)
    return jnp.concatenate(ordered, axis=0)


def over_term(array, term_count):
    parts = [array]
    for flip in range(1, term_count):
        parts.append(exchange(array, "term", flip))
    return parts


def over_chips(array, sectors):
    parts = [array]
    for flip in range(2, sectors, 2):
        parts.append(exchange(array, "sector", flip))
    return parts


def gather(pieces, sectors, term_count):
    if len(pieces) == 1:
        groups = [over_chips(gather_ordered(pieces[0], term_count), sectors)]
    else:
        main = jnp.concatenate(over_term(pieces[0], term_count))
        rest = jnp.concatenate(over_chips(pieces[1], sectors))
        groups = [over_chips(main, sectors), over_term(rest, term_count)]
    arrays = []
    for group in groups:
        arrays += group
        arrays += [exchange(array, "sector", 1) for array in group]
    return arrays


def main_rows(share):
    return share - share // 3 if share % (3 * HEAD) == 0 else share


def place_waves(wave, arrays, place, sectors, term_count):
    size = wave.shape[1]
    share = size // term_count
    cut = main_rows(share)
    chips = sectors // 2
    mains = arrays[:sectors]
    if len(arrays) == sectors:
        cut = share
    for core in range(2):
        for chip in range(chips):
            source = mains[core * chips + chip]
            slot = 2 * chip + core
            if cut == share:
                wave[slot] = source[...]
                continue
            for flip in range(term_count):
                start = pl.multiple_of((place[1] ^ flip) * share, HEAD)
                wave[slot, pl.ds(start, cut), :] = source[flip * cut : (flip + 1) * cut, :]
    left_over = share - cut
    for i, source in enumerate(arrays[sectors:]):
        core, flip = divmod(i, term_count)
        start = pl.multiple_of((place[1] ^ flip) * share + cut, HEAD)
        for chip in range(chips):
            rows = source[chip * left_over : (chip + 1) * left_over, :]
            wave[2 * chip + core, pl.ds(start, left_over), :] = rows


def fold(values):
    rows, columns = values.shape
    down = jnp.sum(values.reshape(rows // SUBLANES, SUBLANES, columns), axis=0)
    return tree_any([down[:, i : i + LANES] for i in range(0, columns, LANES)])


def tree_any(parts):
    total = parts[0]
    for part in parts[1:]:
        total = total + part
    return total


def plan_kernel(normaliser, triples, owner, live, coef, place, table, weights):
    for k in range(triples.shape[1]):
        table[0, k] = triples[0, k]
        table[1, k] = owner[triples[1, k]] ^ place[0]
        table[2, k] = triples[2, k]
        weights[k] = jnp.where(k < live[0, 0], coef[triples[3, k]], 0.0) * normaliser


def plan(normaliser, triples, owner, live, coef, place):
    slots = triples.shape[1]
    return pl.pallas_call(
        functools.partial(plan_kernel, normaliser),
        out_shape=[
            jax.ShapeDtypeStruct((3, slots), jnp.int32),
            jax.ShapeDtypeStruct((slots,), F32),
        ],
        in_specs=[SCALARS] * 5,
        out_specs=[SCALARS] * 2,
        name="plan",
        compiler_params=SMALL_CALL,
    )(triples, owner, live, coef, place)


def load_kernel(left, right, left_near, right_near, sems):
    copies = []
    for i, (far, near) in enumerate(((left, left_near), (right, right_near))):
        copies += [
            pltpu.make_async_copy(far.at[j], near.at[j], sems.at[i, j])
            for j in range(far.shape[0])
        ]
    for copy in copies:
        copy.start()
    for copy in copies:
        copy.wait()


def load(left, right):
    like = jax.ShapeDtypeStruct(left.shape, left.dtype)
    return pl.pallas_call(
        load_kernel,
        out_shape=[like, like],
        in_specs=[FAR] * 2,
        out_specs=[NEAR] * 2,
        scratch_shapes=[pltpu.SemaphoreType.DMA((2, left.shape[0]))],
        name="load",
        compiler_params=pltpu.CompilerParams(vmem_limit_bytes=12 << 20),
    )(left, right)


STATS = 3
PARTS = 3


def spread(values, columns):
    rows = lax.broadcasted_iota(jnp.int32, (HEAD, columns), 0)
    tile = jnp.zeros((HEAD, columns), F32)
    for i, value in enumerate(values):
        rest = value
        for part in range(PARTS):
            high = rest.astype(BF16).astype(F32)
            tile = jnp.where(rows == PARTS * i + part, high, tile)
            rest = rest - high
    return tile


def joined(head, i):
    row = PARTS * i
    return (head[row : row + 1] + head[row + 1 : row + 2]) + head[row + 2 : row + 3]


def apply_kernel(
    sectors,
    term_count,
    count,
    unroll,
    table,
    weights,
    place,
    left,
    right,
    overlap,
    square,
    *rest,
):
    arrays = rest[:count]
    chunks = rest[count : count + term_count]
    wave, total, halves, image = rest[count + term_count :]
    slots = weights.shape[0]
    size = left.shape[1]
    envs = right.shape[0]
    share = size // term_count
    for env in range(envs):
        total[env] = jnp.zeros((size, size), F32)
    place_waves(wave, arrays, place, sectors, term_count)

    def one(k):
        slot = table[2, k]
        total[slot] += weights[k] * jnp.dot(
            left[table[0, k]], wave[table[1, k]], preferred_element_type=F32
        )

    def step(i, carry):
        for u in range(unroll):
            one(i * unroll + u)
        return carry

    lax.fori_loop(0, slots // unroll, step, 0)
    for env in range(envs):
        columns = slice(env * size, (env + 1) * size)
        high = total[env].astype(BF16)
        halves[:size, columns] = high
        halves[size:, columns] = (total[env] - high.astype(F32)).astype(BF16)
    flat = right[...].reshape(envs * size, size)
    both = jnp.dot(halves[...], flat, preferred_element_type=F32)
    image[...] = both[:size] + both[size:]
    inner = jnp.sum(fold(wave[0].astype(F32) * image[...]), keepdims=True)
    head = spread(
        (
            inner,
            jnp.sum(overlap[...], keepdims=True),
            jnp.sum(square[...], keepdims=True),
        ),
        LANES,
    )
    for flip in range(term_count):
        start = pl.multiple_of((place[1] ^ flip) * share, SUBLANES)
        kind = chunks[flip].dtype
        chunks[flip][:HEAD] = head.astype(kind)
        for i in range(size // LANES):
            slab = image[pl.ds(start, share), i * LANES : (i + 1) * LANES]
            chunks[flip][HEAD + i * share : HEAD + (i + 1) * share] = slab.astype(kind)


def apply_local(
    table, weights, place, left, right, overlap, square, arrays, sectors, term_count
):
    slots = weights.shape[0]
    envs, size, _ = left.shape
    share = size // term_count
    unroll = next(u for u in (4, 2, 1) if slots % u == 0)
    kinds = [F32] + [BF16] * (term_count - 1)
    return pl.pallas_call(
        functools.partial(apply_kernel, sectors, term_count, len(arrays), unroll),
        out_shape=[jax.ShapeDtypeStruct((HEAD + size // LANES * share, LANES), kind) for kind in kinds],
        in_specs=[SCALARS] * 3 + [NEAR] * (4 + len(arrays)),
        out_specs=[NEAR] * term_count,
        scratch_shapes=[
            pltpu.VMEM((sectors, size, size), BF16),
            pltpu.VMEM((envs, size, size), F32),
            pltpu.VMEM((2 * size, envs * size), BF16),
            pltpu.VMEM((size, size), F32),
        ],
        name="apply_triples",
        cost_estimate=pl.CostEstimate(
            flops=2 * size**3 * (slots + 2 * envs),
            bytes_accessed=2 * size * size * (2 * envs + sectors + 1),
            transcendentals=0,
        ),
        compiler_params=pltpu.CompilerParams(vmem_limit_bytes=18 << 20),
    )(table, weights, place, left, right, overlap, square, *arrays)


def add_chunks(chunks, applied):
    share = applied.shape[0]
    for i in range(applied.shape[1] // LANES):
        rows = slice(HEAD + i * share, HEAD + (i + 1) * share)
        slab = tree_any([chunk[rows, :].astype(F32) for chunk in chunks])
        applied[:, i * LANES : (i + 1) * LANES] = slab


def collect_kernel(count, *rest):
    chunks, (applied, stats) = rest[:count], rest[count:]
    add_chunks(chunks, applied)
    heads = [chunk[:HEAD, :].astype(F32) for chunk in chunks]
    rows = lax.broadcasted_iota(jnp.int32, (SUBLANES, LANES), 0)
    tile = jnp.zeros((SUBLANES, LANES), F32)
    for i in range(STATS):
        tile = jnp.where(rows == i, tree([joined(head, i) for head in heads]), tile)
    stats[...] = tile


def collect(chunks, shape):
    return pl.pallas_call(
        functools.partial(collect_kernel, len(chunks)),
        out_shape=[
            jax.ShapeDtypeStruct(shape, F32),
            jax.ShapeDtypeStruct((SUBLANES, LANES), F32),
        ],
        in_specs=[NEAR] * len(chunks),
        out_specs=[NEAR] * 2,
        name="collect",
        compiler_params=SMALL_CALL,
    )(*chunks)


def summed(sums):
    rows = sums.shape[0]
    return tree_any([sums[i : i + SUBLANES] for i in range(0, rows, SUBLANES)])


def first_kernel(rows, *out):
    *pieces, overlap, square = out
    held = rows[...]
    rounded = held.astype(BF16)
    store_pieces(pieces, rounded)
    overlap[...] = fold(held * rounded.astype(F32))
    square[...] = fold(held * held)


def store_pieces(pieces, rows):
    start = 0
    for piece in pieces:
        stop = start + piece.shape[0]
        piece[...] = rows[start:stop]
        start = stop


def piece_shapes(share, size):
    cut = main_rows(share)
    counts = (cut, share - cut) if cut < share else (share,)
    return [jax.ShapeDtypeStruct((count, size), BF16) for count in counts]


def first(rows):
    pieces = [jax.ShapeDtypeStruct(rows.shape, BF16)]
    tile = jax.ShapeDtypeStruct((SUBLANES, LANES), F32)
    *pieces, overlap, square = pl.pallas_call(
        first_kernel,
        out_shape=pieces + [tile, tile],
        in_specs=[NEAR],
        out_specs=[NEAR] * (len(pieces) + 2),
        name="first_wave",
        compiler_params=SMALL_CALL,
    )(rows)
    return pieces, overlap, square


def advance_kernel(
    cell_count,
    position,
    beta,
    scale,
    sums,
    applied,
    current,
    previous,
    diagonal,
    following,
    *rest,
):
    *pieces, overlap, square, quotient, scale_out = rest
    stats = summed(sums)
    ratio = stats[:1, :1] / stats[1:2, :1]
    if position > 0:
        mean = stats[2:3, :1] / cell_count
        inverse = 1.0 / jnp.sqrt(mean + EPSILON)
    else:
        inverse = jnp.ones((1, 1), F32)
    held = current[...]
    residual = (applied[...] - ratio * held) * inverse - (beta[position] * scale[:1, :1]) * previous[...]
    scaled = diagonal[...] * residual
    rounded = scaled.astype(BF16)
    following[...] = scaled
    store_pieces(pieces, rounded)
    overlap[...] = fold(scaled * rounded.astype(F32))
    square[...] = fold(scaled * scaled)
    quotient[...] = jnp.broadcast_to(ratio, quotient.shape)
    scale_out[...] = jnp.broadcast_to(inverse, scale_out.shape)


def advance(cell_count, position, beta, scale, sums, applied, current, previous, diagonal):
    tile = jax.ShapeDtypeStruct((SUBLANES, LANES), F32)
    pieces = piece_shapes(*current.shape)
    following, *pieces, overlap, square, quotient, scale = pl.pallas_call(
        functools.partial(advance_kernel, cell_count, position),
        out_shape=[jax.ShapeDtypeStruct(current.shape, F32)] + pieces + [tile] * 4,
        in_specs=[SCALARS] + [NEAR] * 6,
        out_specs=[NEAR] * (5 + len(pieces)),
        name="advance",
        compiler_params=SMALL_CALL,
    )(beta, scale, sums, applied, current, previous, diagonal)
    return following, pieces, overlap, square, quotient, scale


def closing_kernel(
    position, count, beta, scale, current, previous, diagonal, *rest
):
    chunks = rest[:count]
    applied_out, products = rest[count:]
    add_chunks(chunks, applied_out)
    applied = applied_out[...]
    held = current[...]
    weight = diagonal[...]
    direct = weight * applied
    turned = weight * held
    older = weight * ((beta[position] * scale[:1, :1]) * previous[...])
    pairs = (
        (held, applied),
        (held, held),
        (direct, direct),
        (direct, turned),
        (turned, turned),
        (direct, older),
        (turned, older),
        (older, older),
    )
    rows = lax.broadcasted_iota(jnp.int32, (SUBLANES, LANES), 0)
    tile = jnp.zeros((SUBLANES, LANES), F32)
    for i, (a, b) in enumerate(pairs):
        tile = jnp.where(rows == i, jnp.sum(fold(a * b), keepdims=True), tile)
    products[...] = tile


def closing(position, beta, scale, current, previous, diagonal, chunks):
    return pl.pallas_call(
        functools.partial(closing_kernel, position, len(chunks)),
        out_shape=[
            jax.ShapeDtypeStruct(current.shape, F32),
            jax.ShapeDtypeStruct((SUBLANES, LANES), F32),
        ],
        in_specs=[SCALARS] + [NEAR] * (4 + len(chunks)),
        out_specs=[NEAR] * 2,
        name="closing_products",
        compiler_params=SMALL_CALL,
    )(beta, scale, current, previous, diagonal, *chunks)


def final_kernel(
    cell_count,
    position,
    beta,
    scale,
    sums,
    applied,
    current,
    previous,
    diagonal,
    *rest,
):
    earlier, (out, quotients) = rest[:position], rest[position:]

    stats = summed(sums)

    def total(i):
        return stats[i : i + 1, :1]

    ratio = total(0) / total(1)
    inverse = 1.0 / jnp.sqrt(total(1) / cell_count + EPSILON)
    for i, tile in enumerate(earlier):
        quotients[i] = jnp.max(tile[...])
    quotients[position] = jnp.max(ratio)
    inner = total(2) - 2.0 * ratio * total(3) + ratio * ratio * total(4)
    mixed = total(5) - ratio * total(6)
    squares = inverse * inverse * inner - 2.0 * inverse * mixed + total(7)
    norm = 1.0 / jnp.sqrt(squares / cell_count + EPSILON)
    residual = (applied[...] - ratio * current[...]) * inverse
    residual = residual - (beta[position] * scale[:1, :1]) * previous[...]
    out[...] = diagonal[...] * residual * norm


def final(cell_count, position, beta, scale, sums, applied, current, previous, diagonal, earlier):
    return pl.pallas_call(
        functools.partial(final_kernel, cell_count, position),
        out_shape=[
            jax.ShapeDtypeStruct(current.shape, F32),
            jax.ShapeDtypeStruct((position + 1,), F32),
        ],
        in_specs=[SCALARS] + [NEAR] * (6 + position),
        out_specs=[NEAR, SCALARS],
        name="final_vector",
        compiler_params=SMALL_CALL,
    )(beta, scale, sums, applied, current, previous, diagonal, *earlier)


def local(
    x_start,
    x_prev,
    precond,
    left_env,
    right_env,
    triples,
    trip_count,
    term_coef,
    lanczos_beta,
    block_owner,
):
    sectors = lax.axis_size("sector")
    term_count = lax.axis_size("term")
    size = left_env.shape[1]
    cell_count = sectors * size * size
    place = jnp.stack([lax.axis_index("sector"), lax.axis_index("term")]).astype(jnp.int32)

    normaliser = 1.0 / math.sqrt(term_count * triples.shape[0])
    current, previous, diagonal = x_start[0], x_prev[0], precond[0]
    pieces, overlap, square = first(current)
    table, weights = plan(
        normaliser, triples.T, block_owner, trip_count, term_coef, place
    )
    left, right = load(left_env, right_env)
    scale = jnp.ones((SUBLANES, LANES), F32)
    quotients = []
    for position in range(APPS):
        arrays = gather(pieces, sectors, term_count)
        chunks = apply_local(
            table,
            weights,
            place,
            left,
            right,
            overlap,
            square,
            arrays,
            sectors,
            term_count,
        )
        arrived = [chunks[0]]
        for flip in range(1, term_count):
            arrived.append(exchange(chunks[flip], "term", flip))
        if position < APPS - 1:
            applied, stats = collect(arrived, current.shape)
            sums = lax.all_gather(stats, "sector", axis=0, tiled=True)
            following, pieces, overlap, square, quotient, scale_new = advance(
                cell_count,
                position,
                lanczos_beta,
                scale,
                sums,
                applied,
                current,
                previous,
                diagonal,
            )
            previous, current, scale = current, following, scale_new
            quotients.append(quotient)
        else:
            applied, products = closing(
                position, lanczos_beta, scale, current, previous, diagonal, arrived
            )
            products = sum_term(products, term_count)
            sums = lax.all_gather(products, "sector", axis=0, tiled=True)
            current, quotients = final(
                cell_count,
                position,
                lanczos_beta,
                scale,
                sums,
                applied,
                current,
                previous,
                diagonal,
                quotients,
            )
    return current[None], quotients


def solution(mesh):
    placed = (
        P("sector", "term", None),
        P("sector", "term", None),
        P("sector", "term", None),
        P(("sector", "term"), None, None),
        P(("sector", "term"), None, None),
        P(("sector", "term"), None),
        P("sector", "term"),
        P(),
        P(),
        P(),
    )
    return jax.shard_map(
        local,
        mesh=mesh,
        in_specs=placed,
        out_specs=(P("sector", "term", None), P()),
        check_vma=False,
    )
```

```python
import functools
import math

import jax
import jax.numpy as jnp
from jax import lax
from jax.experimental import pallas as pl
from jax.experimental.pallas import tpu as pltpu
from jax.sharding import PartitionSpec as P


APPS = 3
EPSILON = 1e-06

F32 = jnp.float32
BF16 = jnp.bfloat16
SUBLANES = 8
HEAD = 16
LANES = 128

SCALARS = pl.BlockSpec(memory_space=pltpu.SMEM)
NEAR = pl.BlockSpec(memory_space=pltpu.VMEM)
FAR = pl.BlockSpec(memory_space=pltpu.HBM)
SMALL_CALL = pltpu.CompilerParams(vmem_limit_bytes=4 << 20)


def exchange(array, axis, flip):
    count = lax.axis_size(axis)
    return lax.ppermute(array, axis, [(i, i ^ flip) for i in range(count)])


def tree(parts):
    while len(parts) > 1:
        parts = [parts[i] + parts[i + 1] for i in range(0, len(parts), 2)]
    return parts[0]


def exchange_by_core(array, axis, flips):
    sectors, term_count = lax.axis_size("sector"), lax.axis_size("term")
    pairs = []
    for sector in range(sectors):
        for term in range(term_count):
            flip = flips[sector % 2]
            there = (sector ^ flip, term) if axis == "sector" else (sector, term ^ flip)
            pairs.append((sector * term_count + term, there[0] * term_count + there[1]))
    return lax.ppermute(array, ("sector", "term"), pairs)


def sum_over(values, axis, count, unit):
    if count == 1:
        return values
    widest = count - 1
    sums = [values + exchange(values, axis, unit * widest)]
    for flip in range(1, count // 2):
        one = exchange_by_core(values, axis, (unit * flip, unit * (flip ^ widest)))
        sums.append(one + exchange(one, "sector", 1))
    return tree(sums)


def sum_sector(values, sectors):
    values = values + exchange(values, "sector", 1)
    return sum_over(values, "sector", sectors // 2, 2)


def gather_ordered(rows, term_count):
    parts = [rows]
    for flip in range(1, term_count):
        parts.append(exchange(rows, "term", flip))
    me = lax.axis_index("term")
    ordered = []
    for index in range(term_count):
        chosen = parts[0]
        for flip in range(1, term_count):
            chosen = jnp.where((me ^ flip) == index, parts[flip], chosen)
        ordered.append(chosen)
    return jnp.concatenate(ordered, axis=0)


def over_term(array, term_count):
    parts = [array]
    for flip in range(1, term_count):
        parts.append(exchange(array, "term", flip))
    return parts


def over_chips(array, sectors):
    parts = [array]
    for flip in range(2, sectors, 2):
        parts.append(exchange(array, "sector", flip))
    return parts


def gather(pieces, sectors, term_count):
    if len(pieces) == 1:
        groups = [over_chips(gather_ordered(pieces[0], term_count), sectors)]
    else:
        main = jnp.concatenate(over_term(pieces[0], term_count))
        rest = jnp.concatenate(over_chips(pieces[1], sectors))
        groups = [over_chips(main, sectors), over_term(rest, term_count)]
    arrays = []
    for group in groups:
        arrays += group
        arrays += [exchange(array, "sector", 1) for array in group]
    return arrays


def main_rows(share):
    return share - share // 3 if share % (3 * HEAD) == 0 else share


def place_waves(wave, arrays, place, sectors, term_count):
    size = wave.shape[1]
    share = size // term_count
    cut = main_rows(share)
    chips = sectors // 2
    mains = arrays[:sectors]
    if len(arrays) == sectors:
        cut = share
    for core in range(2):
        for chip in range(chips):
            source = mains[core * chips + chip]
            slot = 2 * chip + core
            if cut == share:
                wave[slot] = source[...]
                continue
            for flip in range(term_count):
                start = pl.multiple_of((place[1] ^ flip) * share, HEAD)
                wave[slot, pl.ds(start, cut), :] = source[flip * cut : (flip + 1) * cut, :]
    left_over = share - cut
    for i, source in enumerate(arrays[sectors:]):
        core, flip = divmod(i, term_count)
        start = pl.multiple_of((place[1] ^ flip) * share + cut, HEAD)
        for chip in range(chips):
            rows = source[chip * left_over : (chip + 1) * left_over, :]
            wave[2 * chip + core, pl.ds(start, left_over), :] = rows


def fold(values):
    rows, columns = values.shape
    down = jnp.sum(values.reshape(rows // SUBLANES, SUBLANES, columns), axis=0)
    return tree_any([down[:, i : i + LANES] for i in range(0, columns, LANES)])


def tree_any(parts):
    total = parts[0]
    for part in parts[1:]:
        total = total + part
    return total


def plan_kernel(normaliser, triples, owner, live, coef, place, table, weights):
    for k in range(triples.shape[1]):
        table[0, k] = triples[0, k]
        table[1, k] = owner[triples[1, k]] ^ place[0]
        table[2, k] = triples[2, k]
        weights[k] = jnp.where(k < live[0, 0], coef[triples[3, k]], 0.0) * normaliser


def plan(normaliser, triples, owner, live, coef, place):
    slots = triples.shape[1]
    return pl.pallas_call(
        functools.partial(plan_kernel, normaliser),
        out_shape=[
            jax.ShapeDtypeStruct((3, slots), jnp.int32),
            jax.ShapeDtypeStruct((slots,), F32),
        ],
        in_specs=[SCALARS] * 5,
        out_specs=[SCALARS] * 2,
        name="plan",
        compiler_params=SMALL_CALL,
    )(triples, owner, live, coef, place)


def load_kernel(left, right, left_near, right_near, sems):
    copies = []
    for i, (far, near) in enumerate(((left, left_near), (right, right_near))):
        copies += [
            pltpu.make_async_copy(far.at[j], near.at[j], sems.at[i, j])
            for j in range(far.shape[0])
        ]
    for copy in copies:
        copy.start()
    for copy in copies:
        copy.wait()


def load(left, right):
    like = jax.ShapeDtypeStruct(left.shape, left.dtype)
    return pl.pallas_call(
        load_kernel,
        out_shape=[like, like],
        in_specs=[FAR] * 2,
        out_specs=[NEAR] * 2,
        scratch_shapes=[pltpu.SemaphoreType.DMA((2, left.shape[0]))],
        name="load",
        compiler_params=pltpu.CompilerParams(vmem_limit_bytes=12 << 20),
    )(left, right)


STATS = 3
PARTS = 3


def spread(values, columns):
    rows = lax.broadcasted_iota(jnp.int32, (HEAD, columns), 0)
    tile = jnp.zeros((HEAD, columns), F32)
    for i, value in enumerate(values):
        rest = value
        for part in range(PARTS):
            high = rest.astype(BF16).astype(F32)
            tile = jnp.where(rows == PARTS * i + part, high, tile)
            rest = rest - high
    return tile


def joined(head, i):
    row = PARTS * i
    return (head[row : row + 1] + head[row + 1 : row + 2]) + head[row + 2 : row + 3]


def apply_kernel(
    sectors,
    term_count,
    count,
    unroll,
    table,
    weights,
    place,
    left,
    right,
    overlap,
    square,
    *rest,
):
    arrays = rest[:count]
    chunks = rest[count : count + term_count]
    wave, total, halves, image = rest[count + term_count :]
    slots = weights.shape[0]
    size = left.shape[1]
    envs = right.shape[0]
    share = size // term_count
    for env in range(envs):
        total[env] = jnp.zeros((size, size), F32)
    place_waves(wave, arrays, place, sectors, term_count)

    def one(k):
        slot = table[2, k]
        total[slot] += weights[k] * jnp.dot(
            left[table[0, k]], wave[table[1, k]], preferred_element_type=F32
        )

    def step(i, carry):
        for u in range(unroll):
            one(i * unroll + u)
        return carry

    lax.fori_loop(0, slots // unroll, step, 0)
    for env in range(envs):
        columns = slice(env * size, (env + 1) * size)
        high = total[env].astype(BF16)
        halves[:size, columns] = high
        halves[size:, columns] = (total[env] - high.astype(F32)).astype(BF16)
    flat = right[...].reshape(envs * size, size)
    both = jnp.dot(halves[...], flat, preferred_element_type=F32)
    image[...] = both[:size] + both[size:]
    inner = jnp.sum(fold(wave[0].astype(F32) * image[...]), keepdims=True)
    head = spread(
        (
            inner,
            jnp.sum(overlap[...], keepdims=True),
            jnp.sum(square[...], keepdims=True),
        ),
        LANES,
    )
    for flip in range(term_count):
        start = pl.multiple_of((place[1] ^ flip) * share, SUBLANES)
        kind = chunks[flip].dtype
        chunks[flip][:HEAD] = head.astype(kind)
        for i in range(size // LANES):
            slab = image[pl.ds(start, share), i * LANES : (i + 1) * LANES]
            chunks[flip][HEAD + i * share : HEAD + (i + 1) * share] = slab.astype(kind)


def apply_local(
    table, weights, place, left, right, overlap, square, arrays, sectors, term_count
):
    slots = weights.shape[0]
    envs, size, _ = left.shape
    share = size // term_count
    unroll = next(u for u in (5, 4, 2, 1) if slots % u == 0)
    kinds = [F32] + [BF16] * (term_count - 1)
    return pl.pallas_call(
        functools.partial(apply_kernel, sectors, term_count, len(arrays), unroll),
        out_shape=[jax.ShapeDtypeStruct((HEAD + size // LANES * share, LANES), kind) for kind in kinds],
        in_specs=[SCALARS] * 3 + [NEAR] * (4 + len(arrays)),
        out_specs=[NEAR] * term_count,
        scratch_shapes=[
            pltpu.VMEM((sectors, size, size), BF16),
            pltpu.VMEM((envs, size, size), F32),
            pltpu.VMEM((2 * size, envs * size), BF16),
            pltpu.VMEM((size, size), F32),
        ],
        name="apply_triples",
        cost_estimate=pl.CostEstimate(
            flops=2 * size**3 * (slots + 2 * envs),
            bytes_accessed=2 * size * size * (2 * envs + sectors + 1),
            transcendentals=0,
        ),
        compiler_params=pltpu.CompilerParams(vmem_limit_bytes=18 << 20),
    )(table, weights, place, left, right, overlap, square, *arrays)


def add_chunks(chunks, applied):
    share = applied.shape[0]
    for i in range(applied.shape[1] // LANES):
        rows = slice(HEAD + i * share, HEAD + (i + 1) * share)
        slab = tree_any([chunk[rows, :].astype(F32) for chunk in chunks])
        applied[:, i * LANES : (i + 1) * LANES] = slab


def collect_kernel(count, *rest):
    chunks, (applied, stats) = rest[:count], rest[count:]
    add_chunks(chunks, applied)
    heads = [chunk[:HEAD, :].astype(F32) for chunk in chunks]
    rows = lax.broadcasted_iota(jnp.int32, (SUBLANES, LANES), 0)
    tile = jnp.zeros((SUBLANES, LANES), F32)
    for i in range(STATS):
        tile = jnp.where(rows == i, tree([joined(head, i) for head in heads]), tile)
    stats[...] = tile


def collect(chunks, shape):
    return pl.pallas_call(
        functools.partial(collect_kernel, len(chunks)),
        out_shape=[
            jax.ShapeDtypeStruct(shape, F32),
            jax.ShapeDtypeStruct((SUBLANES, LANES), F32),
        ],
        in_specs=[NEAR] * len(chunks),
        out_specs=[NEAR] * 2,
        name="collect",
        compiler_params=SMALL_CALL,
    )(*chunks)


def first_kernel(rows, *out):
    *pieces, overlap, square = out
    held = rows[...]
    rounded = held.astype(BF16)
    store_pieces(pieces, rounded)
    overlap[...] = fold(held * rounded.astype(F32))
    square[...] = fold(held * held)


def store_pieces(pieces, rows):
    start = 0
    for piece in pieces:
        stop = start + piece.shape[0]
        piece[...] = rows[start:stop]
        start = stop


def piece_shapes(share, size):
    cut = main_rows(share)
    counts = (cut, share - cut) if cut < share else (share,)
    return [jax.ShapeDtypeStruct((count, size), BF16) for count in counts]


def first(rows):
    pieces = [jax.ShapeDtypeStruct(rows.shape, BF16)]
    tile = jax.ShapeDtypeStruct((SUBLANES, LANES), F32)
    *pieces, overlap, square = pl.pallas_call(
        first_kernel,
        out_shape=pieces + [tile, tile],
        in_specs=[NEAR],
        out_specs=[NEAR] * (len(pieces) + 2),
        name="first_wave",
        compiler_params=SMALL_CALL,
    )(rows)
    return pieces, overlap, square


def advance_kernel(
    cell_count,
    position,
    beta,
    scale,
    sums,
    applied,
    current,
    previous,
    diagonal,
    following,
    *rest,
):
    *pieces, overlap, square, quotient, scale_out = rest
    stats = sums[...]
    ratio = stats[:1, :1] / stats[1:2, :1]
    if position > 0:
        mean = stats[2:3, :1] / cell_count
        inverse = 1.0 / jnp.sqrt(mean + EPSILON)
    else:
        inverse = jnp.ones((1, 1), F32)
    held = current[...]
    residual = (applied[...] - ratio * held) * inverse - (beta[position] * scale[:1, :1]) * previous[...]
    scaled = diagonal[...] * residual
    rounded = scaled.astype(BF16)
    following[...] = scaled
    store_pieces(pieces, rounded)
    overlap[...] = fold(scaled * rounded.astype(F32))
    square[...] = fold(scaled * scaled)
    quotient[...] = jnp.broadcast_to(ratio, quotient.shape)
    scale_out[...] = jnp.broadcast_to(inverse, scale_out.shape)


def advance(cell_count, position, beta, scale, sums, applied, current, previous, diagonal):
    tile = jax.ShapeDtypeStruct((SUBLANES, LANES), F32)
    pieces = piece_shapes(*current.shape)
    following, *pieces, overlap, square, quotient, scale = pl.pallas_call(
        functools.partial(advance_kernel, cell_count, position),
        out_shape=[jax.ShapeDtypeStruct(current.shape, F32)] + pieces + [tile] * 4,
        in_specs=[SCALARS] + [NEAR] * 6,
        out_specs=[NEAR] * (5 + len(pieces)),
        name="advance",
        compiler_params=SMALL_CALL,
    )(beta, scale, sums, applied, current, previous, diagonal)
    return following, pieces, overlap, square, quotient, scale


def closing_kernel(
    position, count, beta, scale, current, previous, diagonal, *rest
):
    chunks = rest[:count]
    applied_out, products = rest[count:]
    add_chunks(chunks, applied_out)
    applied = applied_out[...]
    held = current[...]
    weight = diagonal[...]
    direct = weight * applied
    turned = weight * held
    older = weight * ((beta[position] * scale[:1, :1]) * previous[...])
    pairs = (
        (held, applied),
        (held, held),
        (direct, direct),
        (direct, turned),
        (turned, turned),
        (direct, older),
        (turned, older),
        (older, older),
    )
    rows = lax.broadcasted_iota(jnp.int32, (SUBLANES, LANES), 0)
    tile = jnp.zeros((SUBLANES, LANES), F32)
    for i, (a, b) in enumerate(pairs):
        tile = jnp.where(rows == i, jnp.sum(fold(a * b), keepdims=True), tile)
    products[...] = tile


def closing(position, beta, scale, current, previous, diagonal, chunks):
    return pl.pallas_call(
        functools.partial(closing_kernel, position, len(chunks)),
        out_shape=[
            jax.ShapeDtypeStruct(current.shape, F32),
            jax.ShapeDtypeStruct((SUBLANES, LANES), F32),
        ],
        in_specs=[SCALARS] + [NEAR] * (4 + len(chunks)),
        out_specs=[NEAR] * 2,
        name="closing_products",
        compiler_params=SMALL_CALL,
    )(beta, scale, current, previous, diagonal, *chunks)


def final_kernel(
    cell_count,
    position,
    beta,
    scale,
    sums,
    applied,
    current,
    previous,
    diagonal,
    *rest,
):
    earlier, (out, quotients) = rest[:position], rest[position:]

    stats = sums[...]

    def total(i):
        return stats[i : i + 1, :1]

    ratio = total(0) / total(1)
    inverse = 1.0 / jnp.sqrt(total(1) / cell_count + EPSILON)
    for i, tile in enumerate(earlier):
        quotients[i] = jnp.max(tile[...])
    quotients[position] = jnp.max(ratio)
    inner = total(2) - 2.0 * ratio * total(3) + ratio * ratio * total(4)
    mixed = total(5) - ratio * total(6)
    squares = inverse * inverse * inner - 2.0 * inverse * mixed + total(7)
    norm = 1.0 / jnp.sqrt(squares / cell_count + EPSILON)
    residual = (applied[...] - ratio * current[...]) * inverse
    residual = residual - (beta[position] * scale[:1, :1]) * previous[...]
    out[...] = diagonal[...] * residual * norm


def final(cell_count, position, beta, scale, sums, applied, current, previous, diagonal, earlier):
    return pl.pallas_call(
        functools.partial(final_kernel, cell_count, position),
        out_shape=[
            jax.ShapeDtypeStruct(current.shape, F32),
            jax.ShapeDtypeStruct((position + 1,), F32),
        ],
        in_specs=[SCALARS] + [NEAR] * (6 + position),
        out_specs=[NEAR, SCALARS],
        name="final_vector",
        compiler_params=SMALL_CALL,
    )(beta, scale, sums, applied, current, previous, diagonal, *earlier)


def local(
    x_start,
    x_prev,
    precond,
    left_env,
    right_env,
    triples,
    trip_count,
    term_coef,
    lanczos_beta,
    block_owner,
):
    sectors = lax.axis_size("sector")
    term_count = lax.axis_size("term")
    size = left_env.shape[1]
    cell_count = sectors * size * size
    place = jnp.stack([lax.axis_index("sector"), lax.axis_index("term")]).astype(jnp.int32)

    normaliser = 1.0 / math.sqrt(term_count * triples.shape[0])
    current, previous, diagonal = x_start[0], x_prev[0], precond[0]
    pieces, overlap, square = first(current)
    table, weights = plan(
        normaliser, triples.T, block_owner, trip_count, term_coef, place
    )
    left, right = load(left_env, right_env)
    scale = jnp.ones((SUBLANES, LANES), F32)
    quotients = []
    for position in range(APPS):
        arrays = gather(pieces, sectors, term_count)
        chunks = apply_local(
            table,
            weights,
            place,
            left,
            right,
            overlap,
            square,
            arrays,
            sectors,
            term_count,
        )
        arrived = [chunks[0]]
        for flip in range(1, term_count):
            arrived.append(exchange(chunks[flip], "term", flip))
        if position < APPS - 1:
            applied, stats = collect(arrived, current.shape)
            sums = sum_sector(stats, sectors)
            following, pieces, overlap, square, quotient, scale_new = advance(
                cell_count,
                position,
                lanczos_beta,
                scale,
                sums,
                applied,
                current,
                previous,
                diagonal,
            )
            previous, current, scale = current, following, scale_new
            quotients.append(quotient)
        else:
            applied, products = closing(
                position, lanczos_beta, scale, current, previous, diagonal, arrived
            )
            sums = sum_over(sum_sector(products, sectors), "term", term_count, 1)
            current, quotients = final(
                cell_count,
                position,
                lanczos_beta,
                scale,
                sums,
                applied,
                current,
                previous,
                diagonal,
                quotients,
            )
    return current[None], quotients


def solution(mesh):
    placed = (
        P("sector", "term", None),
        P("sector", "term", None),
        P("sector", "term", None),
        P(("sector", "term"), None, None),
        P(("sector", "term"), None, None),
        P(("sector", "term"), None),
        P("sector", "term"),
        P(),
        P(),
        P(),
    )
    return jax.shard_map(
        local,
        mesh=mesh,
        in_specs=placed,
        out_specs=(P("sector", "term", None), P()),
        check_vma=False,
    )
```

```python
import functools
import math

import jax
import jax.numpy as jnp
from jax import lax
from jax.experimental import pallas as pl
from jax.experimental.pallas import tpu as pltpu
from jax.sharding import PartitionSpec as P


APPS = 3
EPSILON = 1e-06

F32 = jnp.float32
BF16 = jnp.bfloat16
SUBLANES = 8
HEAD = 16
LANES = 128

SCALARS = pl.BlockSpec(memory_space=pltpu.SMEM)
NEAR = pl.BlockSpec(memory_space=pltpu.VMEM)
FAR = pl.BlockSpec(memory_space=pltpu.HBM)
SMALL_CALL = pltpu.CompilerParams(vmem_limit_bytes=4 << 20)


def exchange(array, axis, flip):
    count = lax.axis_size(axis)
    return lax.ppermute(array, axis, [(i, i ^ flip) for i in range(count)])


def tree(parts):
    while len(parts) > 1:
        parts = [parts[i] + parts[i + 1] for i in range(0, len(parts), 2)]
    return parts[0]


def exchange_by_core(array, axis, flips):
    sectors, term_count = lax.axis_size("sector"), lax.axis_size("term")
    pairs = []
    for sector in range(sectors):
        for term in range(term_count):
            flip = flips[sector % 2]
            there = (sector ^ flip, term) if axis == "sector" else (sector, term ^ flip)
            pairs.append((sector * term_count + term, there[0] * term_count + there[1]))
    return lax.ppermute(array, ("sector", "term"), pairs)


def sum_over(values, axis, count, unit):
    if count == 1:
        return values
    widest = count - 1
    sums = [values + exchange(values, axis, unit * widest)]
    for flip in range(1, count // 2):
        one = exchange_by_core(values, axis, (unit * flip, unit * (flip ^ widest)))
        sums.append(one + exchange(one, "sector", 1))
    return tree(sums)


def sum_sector(values, sectors):
    values = values + exchange(values, "sector", 1)
    return sum_over(values, "sector", sectors // 2, 2)


def gather_ordered(rows, term_count):
    parts = [rows]
    for flip in range(1, term_count):
        parts.append(exchange(rows, "term", flip))
    me = lax.axis_index("term")
    ordered = []
    for index in range(term_count):
        chosen = parts[0]
        for flip in range(1, term_count):
            chosen = jnp.where((me ^ flip) == index, parts[flip], chosen)
        ordered.append(chosen)
    return jnp.concatenate(ordered, axis=0)


def over_term(array, term_count):
    parts = [array]
    for flip in range(1, term_count):
        parts.append(exchange(array, "term", flip))
    return parts


def over_chips(array, sectors):
    parts = [array]
    for flip in range(2, sectors, 2):
        parts.append(exchange(array, "sector", flip))
    return parts


def gather(rows, sectors, term_count):
    if rows.shape[0] % HEAD:
        own = over_chips(gather_ordered(rows, term_count), sectors)
    else:
        over = over_term(rows, term_count)
        across = over_chips(rows, sectors)[1:]
        near = jnp.concatenate(over + across)
        own = [near]
        if term_count > 1:
            own += over_chips(jnp.concatenate(over[1:]), sectors)[1:]
    swapped = []
    for array in own:
        swapped.append(exchange(array, "sector", 1))
    return own + swapped


def place_waves(wave, arrays, place, sectors, term_count):
    share = wave.shape[1] // term_count
    chips = sectors // 2
    count = len(arrays) // 2

    def put(slot, flip, source, entry):
        start = pl.multiple_of((place[1] ^ flip) * share, HEAD)
        wave[slot, pl.ds(start, share), :] = source[entry * share : (entry + 1) * share, :]

    for core in range(2):
        held = arrays[core * count : (core + 1) * count]
        if share % HEAD:
            for chip in range(chips):
                wave[2 * chip + core] = held[chip][...]
            continue
        for flip in range(term_count):
            put(core, flip, held[0], flip)
        for chip in range(1, chips):
            put(2 * chip + core, 0, held[0], term_count + chip - 1)
            for flip in range(1, term_count):
                put(2 * chip + core, flip, held[chip], flip - 1)


def fold(values):
    rows, columns = values.shape
    down = jnp.sum(values.reshape(rows // SUBLANES, SUBLANES, columns), axis=0)
    return tree_any([down[:, i : i + LANES] for i in range(0, columns, LANES)])


def tree_any(parts):
    total = parts[0]
    for part in parts[1:]:
        total = total + part
    return total


def plan_kernel(normaliser, triples, owner, live, coef, place, table, weights):
    for k in range(triples.shape[1]):
        table[0, k] = triples[0, k]
        table[1, k] = owner[triples[1, k]] ^ place[0]
        table[2, k] = triples[2, k]
        weights[k] = jnp.where(k < live[0, 0], coef[triples[3, k]], 0.0) * normaliser


def plan(normaliser, triples, owner, live, coef, place):
    slots = triples.shape[1]
    return pl.pallas_call(
        functools.partial(plan_kernel, normaliser),
        out_shape=[
            jax.ShapeDtypeStruct((3, slots), jnp.int32),
            jax.ShapeDtypeStruct((slots,), F32),
        ],
        in_specs=[SCALARS] * 5,
        out_specs=[SCALARS] * 2,
        name="plan",
        compiler_params=SMALL_CALL,
    )(triples, owner, live, coef, place)


def load_kernel(left, right, left_near, right_near, sems):
    copies = []
    for i, (far, near) in enumerate(((left, left_near), (right, right_near))):
        copies += [
            pltpu.make_async_copy(far.at[j], near.at[j], sems.at[i, j])
            for j in range(far.shape[0])
        ]
    for copy in copies:
        copy.start()
    for copy in copies:
        copy.wait()


def load(left, right):
    like = jax.ShapeDtypeStruct(left.shape, left.dtype)
    return pl.pallas_call(
        load_kernel,
        out_shape=[like, like],
        in_specs=[FAR] * 2,
        out_specs=[NEAR] * 2,
        scratch_shapes=[pltpu.SemaphoreType.DMA((2, left.shape[0]))],
        name="load",
        compiler_params=pltpu.CompilerParams(vmem_limit_bytes=12 << 20),
    )(left, right)


STATS = 3
PARTS = 3


def spread(values, columns):
    rows = lax.broadcasted_iota(jnp.int32, (HEAD, columns), 0)
    tile = jnp.zeros((HEAD, columns), F32)
    for i, value in enumerate(values):
        rest = value
        for part in range(PARTS):
            high = rest.astype(BF16).astype(F32)
            tile = jnp.where(rows == PARTS * i + part, high, tile)
            rest = rest - high
    return tile


def joined(head, i):
    row = PARTS * i
    return (head[row : row + 1] + head[row + 1 : row + 2]) + head[row + 2 : row + 3]


def apply_kernel(
    sectors,
    term_count,
    count,
    unroll,
    table,
    weights,
    place,
    left,
    right,
    overlap,
    square,
    *rest,
):
    arrays = rest[:count]
    chunks = rest[count : count + term_count]
    wave, total, halves, image = rest[count + term_count :]
    slots = weights.shape[0]
    size = left.shape[1]
    envs = right.shape[0]
    share = size // term_count
    for env in range(envs):
        total[env] = jnp.zeros((size, size), F32)
    place_waves(wave, arrays, place, sectors, term_count)

    def one(k):
        slot = table[2, k]
        total[slot] += weights[k] * jnp.dot(
            left[table[0, k]], wave[table[1, k]], preferred_element_type=F32
        )

    def step(i, carry):
        for u in range(unroll):
            one(i * unroll + u)
        return carry

    lax.fori_loop(0, slots // unroll, step, 0)
    for env in range(envs):
        columns = slice(env * size, (env + 1) * size)
        high = total[env].astype(BF16)
        halves[:size, columns] = high
        halves[size:, columns] = (total[env] - high.astype(F32)).astype(BF16)
    flat = right[...].reshape(envs * size, size)
    both = jnp.dot(halves[...], flat, preferred_element_type=F32)
    image[...] = both[:size] + both[size:]
    inner = jnp.sum(fold(wave[0].astype(F32) * image[...]), keepdims=True)
    head = spread(
        (
            inner,
            jnp.sum(overlap[...], keepdims=True),
            jnp.sum(square[...], keepdims=True),
        ),
        LANES,
    )
    for flip in range(term_count):
        start = pl.multiple_of((place[1] ^ flip) * share, SUBLANES)
        kind = chunks[flip].dtype
        chunks[flip][:HEAD] = head.astype(kind)
        for i in range(size // LANES):
            slab = image[pl.ds(start, share), i * LANES : (i + 1) * LANES]
            chunks[flip][HEAD + i * share : HEAD + (i + 1) * share] = slab.astype(kind)


def apply_local(
    table, weights, place, left, right, overlap, square, arrays, sectors, term_count
):
    slots = weights.shape[0]
    envs, size, _ = left.shape
    share = size // term_count
    unroll = next(u for u in (10, 8, 5, 4, 2, 1) if slots % u == 0)
    kinds = [F32] + [BF16] * (term_count - 1)
    return pl.pallas_call(
        functools.partial(apply_kernel, sectors, term_count, len(arrays), unroll),
        out_shape=[jax.ShapeDtypeStruct((HEAD + size // LANES * share, LANES), kind) for kind in kinds],
        in_specs=[SCALARS] * 3 + [NEAR] * (4 + len(arrays)),
        out_specs=[NEAR] * term_count,
        scratch_shapes=[
            pltpu.VMEM((sectors, size, size), BF16),
            pltpu.VMEM((envs, size, size), F32),
            pltpu.VMEM((2 * size, envs * size), BF16),
            pltpu.VMEM((size, size), F32),
        ],
        name="apply_triples",
        cost_estimate=pl.CostEstimate(
            flops=2 * size**3 * (slots + 2 * envs),
            bytes_accessed=2 * size * size * (2 * envs + sectors + 1),
            transcendentals=0,
        ),
        compiler_params=pltpu.CompilerParams(vmem_limit_bytes=18 << 20),
    )(table, weights, place, left, right, overlap, square, *arrays)


def add_chunks(chunks, applied):
    share = applied.shape[0]
    for i in range(applied.shape[1] // LANES):
        rows = slice(HEAD + i * share, HEAD + (i + 1) * share)
        slab = tree_any([chunk[rows, :].astype(F32) for chunk in chunks])
        applied[:, i * LANES : (i + 1) * LANES] = slab


def collect_kernel(count, *rest):
    chunks, (applied, stats) = rest[:count], rest[count:]
    add_chunks(chunks, applied)
    heads = [chunk[:HEAD, :].astype(F32) for chunk in chunks]
    rows = lax.broadcasted_iota(jnp.int32, (SUBLANES, LANES), 0)
    tile = jnp.zeros((SUBLANES, LANES), F32)
    for i in range(STATS):
        tile = jnp.where(rows == i, tree([joined(head, i) for head in heads]), tile)
    stats[...] = tile


def collect(chunks, shape):
    return pl.pallas_call(
        functools.partial(collect_kernel, len(chunks)),
        out_shape=[
            jax.ShapeDtypeStruct(shape, F32),
            jax.ShapeDtypeStruct((SUBLANES, LANES), F32),
        ],
        in_specs=[NEAR] * len(chunks),
        out_specs=[NEAR] * 2,
        name="collect",
        compiler_params=SMALL_CALL,
    )(*chunks)


def first_kernel(rows, wave, overlap, square):
    held = rows[...]
    rounded = held.astype(BF16)
    wave[...] = rounded
    overlap[...] = fold(held * rounded.astype(F32))
    square[...] = fold(held * held)


def first(rows):
    tile = jax.ShapeDtypeStruct((SUBLANES, LANES), F32)
    return pl.pallas_call(
        first_kernel,
        out_shape=[jax.ShapeDtypeStruct(rows.shape, BF16), tile, tile],
        in_specs=[NEAR],
        out_specs=[NEAR] * 3,
        name="first_wave",
        compiler_params=SMALL_CALL,
    )(rows)


def advance_kernel(
    cell_count,
    position,
    beta,
    scale,
    sums,
    applied,
    current,
    previous,
    diagonal,
    following,
    wave,
    overlap,
    square,
    quotient,
    scale_out,
):
    stats = sums[...]
    ratio = stats[:1, :1] / stats[1:2, :1]
    if position > 0:
        mean = stats[2:3, :1] / cell_count
        inverse = 1.0 / jnp.sqrt(mean + EPSILON)
    else:
        inverse = jnp.ones((1, 1), F32)
    held = current[...]
    residual = (applied[...] - ratio * held) * inverse - (beta[position] * scale[:1, :1]) * previous[...]
    scaled = diagonal[...] * residual
    rounded = scaled.astype(BF16)
    following[...] = scaled
    wave[...] = rounded
    overlap[...] = fold(scaled * rounded.astype(F32))
    square[...] = fold(scaled * scaled)
    quotient[...] = jnp.broadcast_to(ratio, quotient.shape)
    scale_out[...] = jnp.broadcast_to(inverse, scale_out.shape)


def advance(cell_count, position, beta, scale, sums, applied, current, previous, diagonal):
    tile = jax.ShapeDtypeStruct((SUBLANES, LANES), F32)
    rows = jax.ShapeDtypeStruct(current.shape, F32)
    wave = jax.ShapeDtypeStruct(current.shape, BF16)
    return pl.pallas_call(
        functools.partial(advance_kernel, cell_count, position),
        out_shape=[rows, wave] + [tile] * 4,
        in_specs=[SCALARS] + [NEAR] * 6,
        out_specs=[NEAR] * 6,
        name="advance",
        compiler_params=SMALL_CALL,
    )(beta, scale, sums, applied, current, previous, diagonal)


def closing_kernel(
    position, count, beta, scale, current, previous, diagonal, *rest
):
    chunks = rest[:count]
    applied_out, products = rest[count:]
    add_chunks(chunks, applied_out)
    applied = applied_out[...]
    held = current[...]
    weight = diagonal[...]
    direct = weight * applied
    turned = weight * held
    older = weight * ((beta[position] * scale[:1, :1]) * previous[...])
    pairs = (
        (held, applied),
        (held, held),
        (direct, direct),
        (direct, turned),
        (turned, turned),
        (direct, older),
        (turned, older),
        (older, older),
    )
    rows = lax.broadcasted_iota(jnp.int32, (SUBLANES, LANES), 0)
    tile = jnp.zeros((SUBLANES, LANES), F32)
    for i, (a, b) in enumerate(pairs):
        tile = jnp.where(rows == i, jnp.sum(fold(a * b), keepdims=True), tile)
    products[...] = tile


def closing(position, beta, scale, current, previous, diagonal, chunks):
    return pl.pallas_call(
        functools.partial(closing_kernel, position, len(chunks)),
        out_shape=[
            jax.ShapeDtypeStruct(current.shape, F32),
            jax.ShapeDtypeStruct((SUBLANES, LANES), F32),
        ],
        in_specs=[SCALARS] + [NEAR] * (4 + len(chunks)),
        out_specs=[NEAR] * 2,
        name="closing_products",
        compiler_params=SMALL_CALL,
    )(beta, scale, current, previous, diagonal, *chunks)


def final_kernel(
    cell_count,
    position,
    beta,
    scale,
    sums,
    applied,
    current,
    previous,
    diagonal,
    *rest,
):
    earlier, (out, quotients) = rest[:position], rest[position:]

    stats = sums[...]

    def total(i):
        return stats[i : i + 1, :1]

    ratio = total(0) / total(1)
    inverse = 1.0 / jnp.sqrt(total(1) / cell_count + EPSILON)
    for i, tile in enumerate(earlier):
        quotients[i] = jnp.max(tile[...])
    quotients[position] = jnp.max(ratio)
    inner = total(2) - 2.0 * ratio * total(3) + ratio * ratio * total(4)
    mixed = total(5) - ratio * total(6)
    squares = inverse * inverse * inner - 2.0 * inverse * mixed + total(7)
    norm = 1.0 / jnp.sqrt(squares / cell_count + EPSILON)
    residual = (applied[...] - ratio * current[...]) * inverse
    residual = residual - (beta[position] * scale[:1, :1]) * previous[...]
    out[...] = diagonal[...] * residual * norm


def final(cell_count, position, beta, scale, sums, applied, current, previous, diagonal, earlier):
    return pl.pallas_call(
        functools.partial(final_kernel, cell_count, position),
        out_shape=[
            jax.ShapeDtypeStruct(current.shape, F32),
            jax.ShapeDtypeStruct((position + 1,), F32),
        ],
        in_specs=[SCALARS] + [NEAR] * (6 + position),
        out_specs=[NEAR, SCALARS],
        name="final_vector",
        compiler_params=SMALL_CALL,
    )(beta, scale, sums, applied, current, previous, diagonal, *earlier)


def local(
    x_start,
    x_prev,
    precond,
    left_env,
    right_env,
    triples,
    trip_count,
    term_coef,
    lanczos_beta,
    block_owner,
):
    sectors = lax.axis_size("sector")
    term_count = lax.axis_size("term")
    size = left_env.shape[1]
    cell_count = sectors * size * size
    place = jnp.stack([lax.axis_index("sector"), lax.axis_index("term")]).astype(jnp.int32)

    normaliser = 1.0 / math.sqrt(term_count * triples.shape[0])
    current, previous, diagonal = x_start[0], x_prev[0], precond[0]
    rows, overlap, square = first(current)
    table, weights = plan(
        normaliser, triples.T, block_owner, trip_count, term_coef, place
    )
    left, right = load(left_env, right_env)
    scale = jnp.ones((SUBLANES, LANES), F32)
    quotients = []
    for position in range(APPS):
        arrays = gather(rows, sectors, term_count)
        chunks = apply_local(
            table,
            weights,
            place,
            left,
            right,
            overlap,
            square,
            arrays,
            sectors,
            term_count,
        )
        arrived = [chunks[0]]
        for flip in range(1, term_count):
            arrived.append(exchange(chunks[flip], "term", flip))
        if position < APPS - 1:
            applied, stats = collect(arrived, current.shape)
            sums = sum_sector(stats, sectors)
            following, rows, overlap, square, quotient, scale_new = advance(
                cell_count,
                position,
                lanczos_beta,
                scale,
                sums,
                applied,
                current,
                previous,
                diagonal,
            )
            previous, current, scale = current, following, scale_new
            quotients.append(quotient)
        else:
            applied, products = closing(
                position, lanczos_beta, scale, current, previous, diagonal, arrived
            )
            sums = sum_over(sum_sector(products, sectors), "term", term_count, 1)
            current, quotients = final(
                cell_count,
                position,
                lanczos_beta,
                scale,
                sums,
                applied,
                current,
                previous,
                diagonal,
                quotients,
            )
    return current[None], quotients


def solution(mesh):
    placed = (
        P("sector", "term", None),
        P("sector", "term", None),
        P("sector", "term", None),
        P(("sector", "term"), None, None),
        P(("sector", "term"), None, None),
        P(("sector", "term"), None),
        P("sector", "term"),
        P(),
        P(),
        P(),
    )
    return jax.shard_map(
        local,
        mesh=mesh,
        in_specs=placed,
        out_specs=(P("sector", "term", None), P()),
        check_vma=False,
    )
```

```python
import functools
import math

import jax
import jax.numpy as jnp
from jax import lax
from jax.experimental import pallas as pl
from jax.experimental.pallas import tpu as pltpu
from jax.sharding import PartitionSpec as P


APPS = 3
EPSILON = 1e-06

F32 = jnp.float32
BF16 = jnp.bfloat16
SUBLANES = 8
HEAD = 16
LANES = 128

SCALARS = pl.BlockSpec(memory_space=pltpu.SMEM)
NEAR = pl.BlockSpec(memory_space=pltpu.VMEM)
FAR = pl.BlockSpec(memory_space=pltpu.HBM)
SMALL_CALL = pltpu.CompilerParams(vmem_limit_bytes=4 << 20)


def exchange(array, axis, flip):
    count = lax.axis_size(axis)
    return lax.ppermute(array, axis, [(i, i ^ flip) for i in range(count)])


def tree(parts):
    while len(parts) > 1:
        parts = [parts[i] + parts[i + 1] for i in range(0, len(parts), 2)]
    return parts[0]


def exchange_by_core(array, axis, flips):
    sectors, term_count = lax.axis_size("sector"), lax.axis_size("term")
    pairs = []
    for sector in range(sectors):
        for term in range(term_count):
            flip = flips[sector % 2]
            there = (sector ^ flip, term) if axis == "sector" else (sector, term ^ flip)
            pairs.append((sector * term_count + term, there[0] * term_count + there[1]))
    return lax.ppermute(array, ("sector", "term"), pairs)


def sum_over(values, axis, count, unit):
    if count == 1:
        return values
    widest = count - 1
    sums = [values + exchange(values, axis, unit * widest)]
    for flip in range(1, count // 2):
        one = exchange_by_core(values, axis, (unit * flip, unit * (flip ^ widest)))
        sums.append(one + exchange(one, "sector", 1))
    return tree(sums)


def sum_sector(values, sectors):
    values = values + exchange(values, "sector", 1)
    return sum_over(values, "sector", sectors // 2, 2)


def gather_ordered(rows, term_count):
    parts = [rows]
    for flip in range(1, term_count):
        parts.append(exchange(rows, "term", flip))
    me = lax.axis_index("term")
    ordered = []
    for index in range(term_count):
        chosen = parts[0]
        for flip in range(1, term_count):
            chosen = jnp.where((me ^ flip) == index, parts[flip], chosen)
        ordered.append(chosen)
    return jnp.concatenate(ordered, axis=0)


def over_term(array, term_count):
    parts = [array]
    for flip in range(1, term_count):
        parts.append(exchange(array, "term", flip))
    return parts


def over_chips(array, sectors):
    parts = [array]
    for flip in range(2, sectors, 2):
        parts.append(exchange(array, "sector", flip))
    return parts


def gather(rows, sectors, term_count, split):
    if rows.shape[0] % HEAD:
        own = over_chips(gather_ordered(rows, term_count), sectors)
    else:
        over = over_term(rows, term_count)
        across = over_chips(rows, sectors)[1:]
        own = [jnp.concatenate(over + across)]
        if over[1:] and across:
            cut = rows.shape[0] - HEAD * split
            main = jnp.concatenate([array[:cut] for array in over[1:]])
            own += over_chips(main, sectors)[1:]
            if split:
                tail = jnp.concatenate([array[cut:] for array in across])
                own += over_term(tail, term_count)[1:]
    swapped = []
    for array in own:
        swapped.append(exchange(array, "sector", 1))
    return own + swapped


def place_waves(wave, arrays, place, sectors, term_count):
    share = wave.shape[1] // term_count
    chips = sectors // 2
    count = len(arrays) // 2

    split = count > chips
    cut = share - HEAD * split

    def put(slot, flip, source, entry, height, first=0):
        start = pl.multiple_of((place[1] ^ flip) * share + first, HEAD)
        rows = source[entry * height : (entry + 1) * height, :]
        wave[slot, pl.ds(start, height), :] = rows

    for core in range(2):
        held = arrays[core * count : (core + 1) * count]
        if share % HEAD:
            for chip in range(chips):
                wave[2 * chip + core] = held[chip][...]
            continue
        for flip in range(term_count):
            put(core, flip, held[0], flip, share)
        for chip in range(1, chips):
            slot = 2 * chip + core
            put(slot, 0, held[0], term_count + chip - 1, share)
            for flip in range(1, term_count):
                put(slot, flip, held[chip], flip - 1, cut)
                if split:
                    put(slot, flip, held[chips - 1 + flip], chip - 1, HEAD, cut)


def fold(values):
    rows, columns = values.shape
    down = jnp.sum(values.reshape(rows // SUBLANES, SUBLANES, columns), axis=0)
    return tree_any([down[:, i : i + LANES] for i in range(0, columns, LANES)])


def tree_any(parts):
    total = parts[0]
    for part in parts[1:]:
        total = total + part
    return total


def plan_kernel(normaliser, triples, owner, live, coef, place, table, weights, used):
    for env in range(used.shape[0]):
        used[env] = 0
    for k in range(triples.shape[1]):
        table[3, k] = used[triples[2, k]]
        used[triples[2, k]] = 1
        table[0, k] = triples[0, k]
        table[1, k] = owner[triples[1, k]] ^ place[0]
        table[2, k] = triples[2, k]
        weights[k] = jnp.where(k < live[0, 0], coef[triples[3, k]], 0.0) * normaliser


def plan(normaliser, envs, triples, owner, live, coef, place):
    slots = triples.shape[1]
    return pl.pallas_call(
        functools.partial(plan_kernel, normaliser),
        out_shape=[
            jax.ShapeDtypeStruct((4, slots), jnp.int32),
            jax.ShapeDtypeStruct((slots,), F32),
            jax.ShapeDtypeStruct((envs,), jnp.int32),
        ],
        in_specs=[SCALARS] * 5,
        out_specs=[SCALARS] * 3,
        name="plan",
        compiler_params=SMALL_CALL,
    )(triples, owner, live, coef, place)


def load_kernel(left, right, left_near, right_near, sems):
    copies = []
    for i, (far, near) in enumerate(((left, left_near), (right, right_near))):
        copies += [
            pltpu.make_async_copy(far.at[j], near.at[j], sems.at[i, j])
            for j in range(far.shape[0])
        ]
    for copy in copies:
        copy.start()
    for copy in copies:
        copy.wait()


def load(left, right):
    like = jax.ShapeDtypeStruct(left.shape, left.dtype)
    return pl.pallas_call(
        load_kernel,
        out_shape=[like, like],
        in_specs=[FAR] * 2,
        out_specs=[NEAR] * 2,
        scratch_shapes=[pltpu.SemaphoreType.DMA((2, left.shape[0]))],
        name="load",
        compiler_params=pltpu.CompilerParams(vmem_limit_bytes=12 << 20),
    )(left, right)


STATS = 3
PARTS = 3


def spread(values, columns):
    rows = lax.broadcasted_iota(jnp.int32, (HEAD, columns), 0)
    tile = jnp.zeros((HEAD, columns), F32)
    for i, value in enumerate(values):
        rest = value
        for part in range(PARTS):
            high = rest.astype(BF16).astype(F32)
            tile = jnp.where(rows == PARTS * i + part, high, tile)
            rest = rest - high
    return tile


def joined(head, i):
    row = PARTS * i
    return (head[row : row + 1] + head[row + 1 : row + 2]) + head[row + 2 : row + 3]


def apply_kernel(
    sectors,
    term_count,
    count,
    unroll,
    table,
    weights,
    used,
    place,
    left,
    right,
    overlap,
    square,
    *rest,
):
    arrays = rest[:count]
    chunks = rest[count : count + term_count]
    wave, total, halves, image = rest[count + term_count :]
    slots = weights.shape[0]
    size = left.shape[1]
    envs = right.shape[0]
    share = size // term_count
    for env in range(envs):

        @pl.when(used[env] == 0)
        def _():
            total[env] = jnp.zeros((size, size), F32)

    place_waves(wave, arrays, place, sectors, term_count)

    def one(k):
        slot = table[2, k]
        product = jnp.dot(left[table[0, k]], wave[table[1, k]], preferred_element_type=F32)
        before = jnp.where(table[3, k] == 0, 0.0, total[slot])
        total[slot] = before + weights[k] * product

    def step(i, carry):
        for u in range(unroll):
            one(i * unroll + u)
        return carry

    lax.fori_loop(0, slots // unroll, step, 0)
    for env in range(envs):
        columns = slice(env * size, (env + 1) * size)
        high = total[env].astype(BF16)
        halves[:size, columns] = high
        halves[size:, columns] = (total[env] - high.astype(F32)).astype(BF16)
    flat = right[...].reshape(envs * size, size)
    both = jnp.dot(halves[...], flat, preferred_element_type=F32)
    image[...] = both[:size] + both[size:]
    inner = jnp.sum(fold(wave[0].astype(F32) * image[...]), keepdims=True)
    head = spread(
        (
            inner,
            jnp.sum(overlap[...], keepdims=True),
            jnp.sum(square[...], keepdims=True),
        ),
        LANES,
    )
    for flip in range(term_count):
        start = pl.multiple_of((place[1] ^ flip) * share, SUBLANES)
        kind = chunks[flip].dtype
        chunks[flip][:HEAD] = head.astype(kind)
        for i in range(size // LANES):
            slab = image[pl.ds(start, share), i * LANES : (i + 1) * LANES]
            chunks[flip][HEAD + i * share : HEAD + (i + 1) * share] = slab.astype(kind)


def apply_local(steps, place, left, right, overlap, square, arrays, sectors, term_count):
    table, weights, used = steps
    slots = weights.shape[0]
    envs, size, _ = left.shape
    share = size // term_count
    unroll = next(u for u in (10, 8, 5, 4, 2, 1) if slots % u == 0)
    kinds = [F32] + [BF16] * (term_count - 1)
    return pl.pallas_call(
        functools.partial(apply_kernel, sectors, term_count, len(arrays), unroll),
        out_shape=[jax.ShapeDtypeStruct((HEAD + size // LANES * share, LANES), kind) for kind in kinds],
        in_specs=[SCALARS] * 4 + [NEAR] * (4 + len(arrays)),
        out_specs=[NEAR] * term_count,
        scratch_shapes=[
            pltpu.VMEM((sectors, size, size), BF16),
            pltpu.VMEM((envs, size, size), F32),
            pltpu.VMEM((2 * size, envs * size), BF16),
            pltpu.VMEM((size, size), F32),
        ],
        name="apply_triples",
        cost_estimate=pl.CostEstimate(
            flops=2 * size**3 * (slots + 2 * envs),
            bytes_accessed=2 * size * size * (2 * envs + sectors + 1),
            transcendentals=0,
        ),
        compiler_params=pltpu.CompilerParams(vmem_limit_bytes=18 << 20),
    )(table, weights, used, place, left, right, overlap, square, *arrays)


def add_chunks(chunks, applied):
    share = applied.shape[0]
    for i in range(applied.shape[1] // LANES):
        rows = slice(HEAD + i * share, HEAD + (i + 1) * share)
        slab = tree_any([chunk[rows, :].astype(F32) for chunk in chunks])
        applied[:, i * LANES : (i + 1) * LANES] = slab


def collect_kernel(count, *rest):
    chunks, (applied, stats) = rest[:count], rest[count:]
    add_chunks(chunks, applied)
    heads = [chunk[:HEAD, :].astype(F32) for chunk in chunks]
    rows = lax.broadcasted_iota(jnp.int32, (SUBLANES, LANES), 0)
    tile = jnp.zeros((SUBLANES, LANES), F32)
    for i in range(STATS):
        tile = jnp.where(rows == i, tree([joined(head, i) for head in heads]), tile)
    stats[...] = tile


def collect(chunks, shape):
    return pl.pallas_call(
        functools.partial(collect_kernel, len(chunks)),
        out_shape=[
            jax.ShapeDtypeStruct(shape, F32),
            jax.ShapeDtypeStruct((SUBLANES, LANES), F32),
        ],
        in_specs=[NEAR] * len(chunks),
        out_specs=[NEAR] * 2,
        name="collect",
        compiler_params=SMALL_CALL,
    )(*chunks)


def first_kernel(rows, wave, overlap, square):
    held = rows[...]
    rounded = held.astype(BF16)
    wave[...] = rounded
    overlap[...] = fold(held * rounded.astype(F32))
    square[...] = fold(held * held)


def first(rows):
    tile = jax.ShapeDtypeStruct((SUBLANES, LANES), F32)
    return pl.pallas_call(
        first_kernel,
        out_shape=[jax.ShapeDtypeStruct(rows.shape, BF16), tile, tile],
        in_specs=[NEAR],
        out_specs=[NEAR] * 3,
        name="first_wave",
        compiler_params=SMALL_CALL,
    )(rows)


def advance_kernel(
    cell_count,
    position,
    beta,
    scale,
    sums,
    applied,
    current,
    previous,
    diagonal,
    following,
    wave,
    overlap,
    square,
    quotient,
    scale_out,
):
    stats = sums[...]
    ratio = stats[:1, :1] / stats[1:2, :1]
    if position > 0:
        mean = stats[2:3, :1] / cell_count
        inverse = 1.0 / jnp.sqrt(mean + EPSILON)
    else:
        inverse = jnp.ones((1, 1), F32)
    held = current[...]
    residual = (applied[...] - ratio * held) * inverse - (beta[position] * scale[:1, :1]) * previous[...]
    scaled = diagonal[...] * residual
    rounded = scaled.astype(BF16)
    following[...] = scaled
    wave[...] = rounded
    overlap[...] = fold(scaled * rounded.astype(F32))
    square[...] = fold(scaled * scaled)
    quotient[...] = jnp.broadcast_to(ratio, quotient.shape)
    scale_out[...] = jnp.broadcast_to(inverse, scale_out.shape)


def advance(cell_count, position, beta, scale, sums, applied, current, previous, diagonal):
    tile = jax.ShapeDtypeStruct((SUBLANES, LANES), F32)
    rows = jax.ShapeDtypeStruct(current.shape, F32)
    wave = jax.ShapeDtypeStruct(current.shape, BF16)
    return pl.pallas_call(
        functools.partial(advance_kernel, cell_count, position),
        out_shape=[rows, wave] + [tile] * 4,
        in_specs=[SCALARS] + [NEAR] * 6,
        out_specs=[NEAR] * 6,
        name="advance",
        compiler_params=SMALL_CALL,
    )(beta, scale, sums, applied, current, previous, diagonal)


def closing_kernel(
    position, count, beta, scale, current, previous, diagonal, *rest
):
    chunks = rest[:count]
    applied_out, products = rest[count:]
    add_chunks(chunks, applied_out)
    applied = applied_out[...]
    held = current[...]
    weight = diagonal[...]
    direct = weight * applied
    turned = weight * held
    older = weight * ((beta[position] * scale[:1, :1]) * previous[...])
    pairs = (
        (held, applied),
        (held, held),
        (direct, direct),
        (direct, turned),
        (turned, turned),
        (direct, older),
        (turned, older),
        (older, older),
    )
    rows = lax.broadcasted_iota(jnp.int32, (SUBLANES, LANES), 0)
    tile = jnp.zeros((SUBLANES, LANES), F32)
    for i, (a, b) in enumerate(pairs):
        tile = jnp.where(rows == i, jnp.sum(fold(a * b), keepdims=True), tile)
    products[...] = tile


def closing(position, beta, scale, current, previous, diagonal, chunks):
    return pl.pallas_call(
        functools.partial(closing_kernel, position, len(chunks)),
        out_shape=[
            jax.ShapeDtypeStruct(current.shape, F32),
            jax.ShapeDtypeStruct((SUBLANES, LANES), F32),
        ],
        in_specs=[SCALARS] + [NEAR] * (4 + len(chunks)),
        out_specs=[NEAR] * 2,
        name="closing_products",
        compiler_params=SMALL_CALL,
    )(beta, scale, current, previous, diagonal, *chunks)


def final_kernel(
    cell_count,
    position,
    beta,
    scale,
    sums,
    applied,
    current,
    previous,
    diagonal,
    *rest,
):
    earlier, (out, quotients) = rest[:position], rest[position:]

    stats = sums[...]

    def total(i):
        return stats[i : i + 1, :1]

    ratio = total(0) / total(1)
    inverse = 1.0 / jnp.sqrt(total(1) / cell_count + EPSILON)
    for i, tile in enumerate(earlier):
        quotients[i] = jnp.max(tile[...])
    quotients[position] = jnp.max(ratio)
    inner = total(2) - 2.0 * ratio * total(3) + ratio * ratio * total(4)
    mixed = total(5) - ratio * total(6)
    squares = inverse * inverse * inner - 2.0 * inverse * mixed + total(7)
    norm = 1.0 / jnp.sqrt(squares / cell_count + EPSILON)
    residual = (applied[...] - ratio * current[...]) * inverse
    residual = residual - (beta[position] * scale[:1, :1]) * previous[...]
    out[...] = diagonal[...] * residual * norm


def final(cell_count, position, beta, scale, sums, applied, current, previous, diagonal, earlier):
    return pl.pallas_call(
        functools.partial(final_kernel, cell_count, position),
        out_shape=[
            jax.ShapeDtypeStruct(current.shape, F32),
            jax.ShapeDtypeStruct((position + 1,), F32),
        ],
        in_specs=[SCALARS] + [NEAR] * (6 + position),
        out_specs=[NEAR, SCALARS],
        name="final_vector",
        compiler_params=SMALL_CALL,
    )(beta, scale, sums, applied, current, previous, diagonal, *earlier)


def local(
    x_start,
    x_prev,
    precond,
    left_env,
    right_env,
    triples,
    trip_count,
    term_coef,
    lanczos_beta,
    block_owner,
):
    sectors = lax.axis_size("sector")
    term_count = lax.axis_size("term")
    size = left_env.shape[1]
    cell_count = sectors * size * size
    place = jnp.stack([lax.axis_index("sector"), lax.axis_index("term")]).astype(jnp.int32)

    normaliser = 1.0 / math.sqrt(term_count * triples.shape[0])
    current, previous, diagonal = x_start[0], x_prev[0], precond[0]
    rows, overlap, square = first(current)
    steps = plan(
        normaliser,
        left_env.shape[0],
        triples.T, block_owner, trip_count, term_coef, place
    )
    left, right = load(left_env, right_env)
    scale = jnp.ones((SUBLANES, LANES), F32)
    quotients = []
    for position in range(APPS):
        arrays = gather(rows, sectors, term_count, position > 0)
        chunks = apply_local(
            steps,
            place,
            left,
            right,
            overlap,
            square,
            arrays,
            sectors,
            term_count,
        )
        arrived = [chunks[0]]
        for flip in range(1, term_count):
            arrived.append(exchange(chunks[flip], "term", flip))
        if position < APPS - 1:
            applied, stats = collect(arrived, current.shape)
            sums = sum_sector(stats, sectors)
            following, rows, overlap, square, quotient, scale_new = advance(
                cell_count,
                position,
                lanczos_beta,
                scale,
                sums,
                applied,
                current,
                previous,
                diagonal,
            )
            previous, current, scale = current, following, scale_new
            quotients.append(quotient)
        else:
            applied, products = closing(
                position, lanczos_beta, scale, current, previous, diagonal, arrived
            )
            sums = sum_over(sum_sector(products, sectors), "term", term_count, 1)
            current, quotients = final(
                cell_count,
                position,
                lanczos_beta,
                scale,
                sums,
                applied,
                current,
                previous,
                diagonal,
                quotients,
            )
    return current[None], quotients


def solution(mesh):
    placed = (
        P("sector", "term", None),
        P("sector", "term", None),
        P("sector", "term", None),
        P(("sector", "term"), None, None),
        P(("sector", "term"), None, None),
        P(("sector", "term"), None),
        P("sector", "term"),
        P(),
        P(),
        P(),
    )
    return jax.shard_map(
        local,
        mesh=mesh,
        in_specs=placed,
        out_specs=(P("sector", "term", None), P()),
        check_vma=False,
    )
```

```python
import functools
import math

import jax
import jax.numpy as jnp
from jax import lax
from jax.experimental import pallas as pl
from jax.experimental.pallas import tpu as pltpu
from jax.sharding import PartitionSpec as P


APPS = 3
EPSILON = 1e-06

F32 = jnp.float32
BF16 = jnp.bfloat16
SUBLANES = 8
HEAD = 16
LANES = 128

SCALARS = pl.BlockSpec(memory_space=pltpu.SMEM)
NEAR = pl.BlockSpec(memory_space=pltpu.VMEM)
FAR = pl.BlockSpec(memory_space=pltpu.HBM)
SMALL_CALL = pltpu.CompilerParams(vmem_limit_bytes=4 << 20)


def exchange(array, axis, flip):
    count = lax.axis_size(axis)
    return lax.ppermute(array, axis, [(i, i ^ flip) for i in range(count)])


def tree(parts):
    while len(parts) > 1:
        parts = [parts[i] + parts[i + 1] for i in range(0, len(parts), 2)]
    return parts[0]


def exchange_by_core(array, axis, flips):
    sectors, term_count = lax.axis_size("sector"), lax.axis_size("term")
    pairs = []
    for sector in range(sectors):
        for term in range(term_count):
            flip = flips[sector % 2]
            there = (sector ^ flip, term) if axis == "sector" else (sector, term ^ flip)
            pairs.append((sector * term_count + term, there[0] * term_count + there[1]))
    return lax.ppermute(array, ("sector", "term"), pairs)


def sum_over(values, axis, count, unit):
    if count == 1:
        return values
    widest = count - 1
    sums = [values + exchange(values, axis, unit * widest)]
    for flip in range(1, count // 2):
        one = exchange_by_core(values, axis, (unit * flip, unit * (flip ^ widest)))
        sums.append(one + exchange(one, "sector", 1))
    return tree(sums)


def sum_sector(values, sectors):
    values = values + exchange(values, "sector", 1)
    return sum_over(values, "sector", sectors // 2, 2)


def gather_ordered(rows, term_count):
    parts = [rows]
    for flip in range(1, term_count):
        parts.append(exchange(rows, "term", flip))
    me = lax.axis_index("term")
    ordered = []
    for index in range(term_count):
        chosen = parts[0]
        for flip in range(1, term_count):
            chosen = jnp.where((me ^ flip) == index, parts[flip], chosen)
        ordered.append(chosen)
    return jnp.concatenate(ordered, axis=0)


def over_term(array, term_count):
    parts = [array]
    for flip in range(1, term_count):
        parts.append(exchange(array, "term", flip))
    return parts


def over_chips(array, sectors):
    parts = [array]
    for flip in range(2, sectors, 2):
        parts.append(exchange(array, "sector", flip))
    return parts


def gather(rows, sectors, term_count, split):
    if rows.shape[0] % HEAD:
        own = over_chips(gather_ordered(rows, term_count), sectors)
    else:
        over = over_term(rows, term_count)
        across = over_chips(rows, sectors)[1:]
        own = [jnp.concatenate(over + across)]
        if over[1:] and across:
            cut = rows.shape[0] - HEAD * split
            main = jnp.concatenate([array[:cut] for array in over[1:]])
            own += over_chips(main, sectors)[1:]
            if split:
                tail = jnp.concatenate([array[cut:] for array in across])
                own.append(jnp.concatenate(over_term(tail, term_count)[1:]))
    swapped = []
    for array in own:
        swapped.append(exchange(array, "sector", 1))
    return own + swapped


def place_waves(wave, arrays, place, sectors, term_count):
    share = wave.shape[1] // term_count
    chips = sectors // 2
    count = len(arrays) // 2

    split = count > chips
    cut = share - HEAD * split

    def put(slot, flip, source, entry, height, first=0):
        start = pl.multiple_of((place[1] ^ flip) * share + first, HEAD)
        rows = source[entry * height : (entry + 1) * height, :]
        wave[slot, pl.ds(start, height), :] = rows

    for core in range(2):
        held = arrays[core * count : (core + 1) * count]
        if share % HEAD:
            for chip in range(chips):
                wave[2 * chip + core] = held[chip][...]
            continue
        for flip in range(term_count):
            put(core, flip, held[0], flip, share)
        for chip in range(1, chips):
            slot = 2 * chip + core
            put(slot, 0, held[0], term_count + chip - 1, share)
            for flip in range(1, term_count):
                put(slot, flip, held[chip], flip - 1, cut)
                if split:
                    entry = (flip - 1) * (chips - 1) + chip - 1
                    put(slot, flip, held[chips], entry, HEAD, cut)


def fold(values):
    rows, columns = values.shape
    down = jnp.sum(values.reshape(rows // SUBLANES, SUBLANES, columns), axis=0)
    return tree_any([down[:, i : i + LANES] for i in range(0, columns, LANES)])


def tree_any(parts):
    total = parts[0]
    for part in parts[1:]:
        total = total + part
    return total


def plan_kernel(normaliser, triples, owner, live, coef, place, table, weights, used):
    for env in range(used.shape[0]):
        used[env] = 0
    for k in range(triples.shape[1]):
        table[3, k] = used[triples[2, k]]
        used[triples[2, k]] = 1
        table[0, k] = triples[0, k]
        table[1, k] = owner[triples[1, k]] ^ place[0]
        table[2, k] = triples[2, k]
        weights[k] = jnp.where(k < live[0, 0], coef[triples[3, k]], 0.0) * normaliser


def plan(normaliser, envs, triples, owner, live, coef, place):
    slots = triples.shape[1]
    return pl.pallas_call(
        functools.partial(plan_kernel, normaliser),
        out_shape=[
            jax.ShapeDtypeStruct((4, slots), jnp.int32),
            jax.ShapeDtypeStruct((slots,), F32),
            jax.ShapeDtypeStruct((envs,), jnp.int32),
        ],
        in_specs=[SCALARS] * 5,
        out_specs=[SCALARS] * 3,
        name="plan",
        compiler_params=SMALL_CALL,
    )(triples, owner, live, coef, place)


def load_kernel(left, right, left_near, right_near, sems):
    copies = []
    for i, (far, near) in enumerate(((left, left_near), (right, right_near))):
        copies += [
            pltpu.make_async_copy(far.at[j], near.at[j], sems.at[i, j])
            for j in range(far.shape[0])
        ]
    for copy in copies:
        copy.start()
    for copy in copies:
        copy.wait()


def load(left, right):
    like = jax.ShapeDtypeStruct(left.shape, left.dtype)
    return pl.pallas_call(
        load_kernel,
        out_shape=[like, like],
        in_specs=[FAR] * 2,
        out_specs=[NEAR] * 2,
        scratch_shapes=[pltpu.SemaphoreType.DMA((2, left.shape[0]))],
        name="load",
        compiler_params=pltpu.CompilerParams(vmem_limit_bytes=12 << 20),
    )(left, right)


STATS = 3
PARTS = 3


def spread(values, columns):
    rows = lax.broadcasted_iota(jnp.int32, (HEAD, columns), 0)
    tile = jnp.zeros((HEAD, columns), F32)
    for i, value in enumerate(values):
        rest = value
        for part in range(PARTS):
            high = rest.astype(BF16).astype(F32)
            tile = jnp.where(rows == PARTS * i + part, high, tile)
            rest = rest - high
    return tile


def joined(head, i):
    row = PARTS * i
    return (head[row : row + 1] + head[row + 1 : row + 2]) + head[row + 2 : row + 3]


def apply_kernel(
    sectors,
    term_count,
    count,
    unroll,
    table,
    weights,
    used,
    place,
    left,
    right,
    overlap,
    square,
    *rest,
):
    arrays = rest[:count]
    chunks = rest[count : count + term_count]
    wave, total, halves, image = rest[count + term_count :]
    slots = weights.shape[0]
    size = left.shape[1]
    envs = right.shape[0]
    share = size // term_count
    for env in range(envs):

        @pl.when(used[env] == 0)
        def _():
            total[env] = jnp.zeros((size, size), F32)

    place_waves(wave, arrays, place, sectors, term_count)

    def one(k):
        slot = table[2, k]
        product = jnp.dot(left[table[0, k]], wave[table[1, k]], preferred_element_type=F32)
        before = jnp.where(table[3, k] == 0, 0.0, total[slot])
        total[slot] = before + weights[k] * product

    def step(i, carry):
        for u in range(unroll):
            one(i * unroll + u)
        return carry

    lax.fori_loop(0, slots // unroll, step, 0)
    for env in range(envs):
        columns = slice(env * size, (env + 1) * size)
        high = total[env].astype(BF16)
        halves[:size, columns] = high
        halves[size:, columns] = (total[env] - high.astype(F32)).astype(BF16)
    flat = right[...].reshape(envs * size, size)
    both = jnp.dot(halves[...], flat, preferred_element_type=F32)
    image[...] = both[:size] + both[size:]
    inner = jnp.sum(fold(wave[0].astype(F32) * image[...]), keepdims=True)
    head = spread(
        (
            inner,
            jnp.sum(overlap[...], keepdims=True),
            jnp.sum(square[...], keepdims=True),
        ),
        LANES,
    )
    for flip in range(term_count):
        start = pl.multiple_of((place[1] ^ flip) * share, SUBLANES)
        kind = chunks[flip].dtype
        chunks[flip][:HEAD] = head.astype(kind)
        for i in range(size // LANES):
            slab = image[pl.ds(start, share), i * LANES : (i + 1) * LANES]
            chunks[flip][HEAD + i * share : HEAD + (i + 1) * share] = slab.astype(kind)


def apply_local(steps, place, left, right, overlap, square, arrays, sectors, term_count):
    table, weights, used = steps
    slots = weights.shape[0]
    envs, size, _ = left.shape
    share = size // term_count
    unroll = next(u for u in (10, 8, 5, 4, 2, 1) if slots % u == 0)
    kinds = [F32] + [BF16] * (term_count - 1)
    return pl.pallas_call(
        functools.partial(apply_kernel, sectors, term_count, len(arrays), unroll),
        out_shape=[jax.ShapeDtypeStruct((HEAD + size // LANES * share, LANES), kind) for kind in kinds],
        in_specs=[SCALARS] * 4 + [NEAR] * (4 + len(arrays)),
        out_specs=[NEAR] * term_count,
        scratch_shapes=[
            pltpu.VMEM((sectors, size, size), BF16),
            pltpu.VMEM((envs, size, size), F32),
            pltpu.VMEM((2 * size, envs * size), BF16),
            pltpu.VMEM((size, size), F32),
        ],
        name="apply_triples",
        cost_estimate=pl.CostEstimate(
            flops=2 * size**3 * (slots + 2 * envs),
            bytes_accessed=2 * size * size * (2 * envs + sectors + 1),
            transcendentals=0,
        ),
        compiler_params=pltpu.CompilerParams(vmem_limit_bytes=18 << 20),
    )(table, weights, used, place, left, right, overlap, square, *arrays)


def add_chunks(chunks, applied):
    share = applied.shape[0]
    for i in range(applied.shape[1] // LANES):
        rows = slice(HEAD + i * share, HEAD + (i + 1) * share)
        slab = tree_any([chunk[rows, :].astype(F32) for chunk in chunks])
        applied[:, i * LANES : (i + 1) * LANES] = slab


def collect_kernel(count, *rest):
    chunks, (applied, stats) = rest[:count], rest[count:]
    add_chunks(chunks, applied)
    heads = [chunk[:HEAD, :].astype(F32) for chunk in chunks]
    rows = lax.broadcasted_iota(jnp.int32, (SUBLANES, LANES), 0)
    tile = jnp.zeros((SUBLANES, LANES), F32)
    for i in range(STATS):
        tile = jnp.where(rows == i, tree([joined(head, i) for head in heads]), tile)
    stats[...] = tile


def collect(chunks, shape):
    return pl.pallas_call(
        functools.partial(collect_kernel, len(chunks)),
        out_shape=[
            jax.ShapeDtypeStruct(shape, F32),
            jax.ShapeDtypeStruct((SUBLANES, LANES), F32),
        ],
        in_specs=[NEAR] * len(chunks),
        out_specs=[NEAR] * 2,
        name="collect",
        compiler_params=SMALL_CALL,
    )(*chunks)


def first_kernel(rows, wave, overlap, square):
    held = rows[...]
    rounded = held.astype(BF16)
    wave[...] = rounded
    overlap[...] = fold(held * rounded.astype(F32))
    square[...] = fold(held * held)


def first(rows):
    tile = jax.ShapeDtypeStruct((SUBLANES, LANES), F32)
    return pl.pallas_call(
        first_kernel,
        out_shape=[jax.ShapeDtypeStruct(rows.shape, BF16), tile, tile],
        in_specs=[NEAR],
        out_specs=[NEAR] * 3,
        name="first_wave",
        compiler_params=SMALL_CALL,
    )(rows)


def advance_kernel(
    cell_count,
    position,
    beta,
    scale,
    sums,
    applied,
    current,
    previous,
    diagonal,
    following,
    wave,
    overlap,
    square,
    quotient,
    scale_out,
):
    stats = sums[...]
    ratio = stats[:1, :1] / stats[1:2, :1]
    if position > 0:
        mean = stats[2:3, :1] / cell_count
        inverse = 1.0 / jnp.sqrt(mean + EPSILON)
    else:
        inverse = jnp.ones((1, 1), F32)
    held = current[...]
    residual = (applied[...] - ratio * held) * inverse - (beta[position] * scale[:1, :1]) * previous[...]
    scaled = diagonal[...] * residual
    rounded = scaled.astype(BF16)
    following[...] = scaled
    wave[...] = rounded
    overlap[...] = fold(scaled * rounded.astype(F32))
    square[...] = fold(scaled * scaled)
    quotient[...] = jnp.broadcast_to(ratio, quotient.shape)
    scale_out[...] = jnp.broadcast_to(inverse, scale_out.shape)


def advance(cell_count, position, beta, scale, sums, applied, current, previous, diagonal):
    tile = jax.ShapeDtypeStruct((SUBLANES, LANES), F32)
    rows = jax.ShapeDtypeStruct(current.shape, F32)
    wave = jax.ShapeDtypeStruct(current.shape, BF16)
    return pl.pallas_call(
        functools.partial(advance_kernel, cell_count, position),
        out_shape=[rows, wave] + [tile] * 4,
        in_specs=[SCALARS] + [NEAR] * 6,
        out_specs=[NEAR] * 6,
        name="advance",
        compiler_params=SMALL_CALL,
    )(beta, scale, sums, applied, current, previous, diagonal)


def closing_kernel(
    position, count, beta, scale, current, previous, diagonal, *rest
):
    chunks = rest[:count]
    applied_out, products = rest[count:]
    add_chunks(chunks, applied_out)
    applied = applied_out[...]
    held = current[...]
    weight = diagonal[...]
    direct = weight * applied
    turned = weight * held
    older = weight * ((beta[position] * scale[:1, :1]) * previous[...])
    pairs = (
        (held, applied),
        (held, held),
        (direct, direct),
        (direct, turned),
        (turned, turned),
        (direct, older),
        (turned, older),
        (older, older),
    )
    rows = lax.broadcasted_iota(jnp.int32, (SUBLANES, LANES), 0)
    tile = jnp.zeros((SUBLANES, LANES), F32)
    for i, (a, b) in enumerate(pairs):
        tile = jnp.where(rows == i, jnp.sum(fold(a * b), keepdims=True), tile)
    products[...] = tile


def closing(position, beta, scale, current, previous, diagonal, chunks):
    return pl.pallas_call(
        functools.partial(closing_kernel, position, len(chunks)),
        out_shape=[
            jax.ShapeDtypeStruct(current.shape, F32),
            jax.ShapeDtypeStruct((SUBLANES, LANES), F32),
        ],
        in_specs=[SCALARS] + [NEAR] * (4 + len(chunks)),
        out_specs=[NEAR] * 2,
        name="closing_products",
        compiler_params=SMALL_CALL,
    )(beta, scale, current, previous, diagonal, *chunks)


def final_kernel(
    cell_count,
    position,
    beta,
    scale,
    sums,
    applied,
    current,
    previous,
    diagonal,
    *rest,
):
    earlier, (out, quotients) = rest[:position], rest[position:]

    stats = sums[...]

    def total(i):
        return stats[i : i + 1, :1]

    ratio = total(0) / total(1)
    inverse = 1.0 / jnp.sqrt(total(1) / cell_count + EPSILON)
    for i, tile in enumerate(earlier):
        quotients[i] = jnp.max(tile[...])
    quotients[position] = jnp.max(ratio)
    inner = total(2) - 2.0 * ratio * total(3) + ratio * ratio * total(4)
    mixed = total(5) - ratio * total(6)
    squares = inverse * inverse * inner - 2.0 * inverse * mixed + total(7)
    norm = 1.0 / jnp.sqrt(squares / cell_count + EPSILON)
    residual = (applied[...] - ratio * current[...]) * inverse
    residual = residual - (beta[position] * scale[:1, :1]) * previous[...]
    out[...] = diagonal[...] * residual * norm


def final(cell_count, position, beta, scale, sums, applied, current, previous, diagonal, earlier):
    return pl.pallas_call(
        functools.partial(final_kernel, cell_count, position),
        out_shape=[
            jax.ShapeDtypeStruct(current.shape, F32),
            jax.ShapeDtypeStruct((position + 1,), F32),
        ],
        in_specs=[SCALARS] + [NEAR] * (6 + position),
        out_specs=[NEAR, SCALARS],
        name="final_vector",
        compiler_params=SMALL_CALL,
    )(beta, scale, sums, applied, current, previous, diagonal, *earlier)


def local(
    x_start,
    x_prev,
    precond,
    left_env,
    right_env,
    triples,
    trip_count,
    term_coef,
    lanczos_beta,
    block_owner,
):
    sectors = lax.axis_size("sector")
    term_count = lax.axis_size("term")
    size = left_env.shape[1]
    cell_count = sectors * size * size
    place = jnp.stack([lax.axis_index("sector"), lax.axis_index("term")]).astype(jnp.int32)

    normaliser = 1.0 / math.sqrt(term_count * triples.shape[0])
    current, previous, diagonal = x_start[0], x_prev[0], precond[0]
    rows, overlap, square = first(current)
    steps = plan(
        normaliser,
        left_env.shape[0],
        triples.T, block_owner, trip_count, term_coef, place
    )
    left, right = load(left_env, right_env)
    scale = jnp.ones((SUBLANES, LANES), F32)
    quotients = []
    for position in range(APPS):
        arrays = gather(rows, sectors, term_count, position > 0)
        chunks = apply_local(
            steps,
            place,
            left,
            right,
            overlap,
            square,
            arrays,
            sectors,
            term_count,
        )
        arrived = [chunks[0]]
        for flip in range(1, term_count):
            arrived.append(exchange(chunks[flip], "term", flip))
        if position < APPS - 1:
            applied, stats = collect(arrived, current.shape)
            sums = sum_sector(stats, sectors)
            following, rows, overlap, square, quotient, scale_new = advance(
                cell_count,
                position,
                lanczos_beta,
                scale,
                sums,
                applied,
                current,
                previous,
                diagonal,
            )
            previous, current, scale = current, following, scale_new
            quotients.append(quotient)
        else:
            applied, products = closing(
                position, lanczos_beta, scale, current, previous, diagonal, arrived
            )
            sums = sum_over(sum_sector(products, sectors), "term", term_count, 1)
            current, quotients = final(
                cell_count,
                position,
                lanczos_beta,
                scale,
                sums,
                applied,
                current,
                previous,
                diagonal,
                quotients,
            )
    return current[None], quotients


def solution(mesh):
    placed = (
        P("sector", "term", None),
        P("sector", "term", None),
        P("sector", "term", None),
        P(("sector", "term"), None, None),
        P(("sector", "term"), None, None),
        P(("sector", "term"), None),
        P("sector", "term"),
        P(),
        P(),
        P(),
    )
    return jax.shard_map(
        local,
        mesh=mesh,
        in_specs=placed,
        out_specs=(P("sector", "term", None), P()),
        check_vma=False,
    )
```
